256 devices in a mesh: tm: 32 (over y, x, core), row: 8 (over z).
Axes of the slice: x: 4, y: 4, z: 8, core: 2. Of those that a mesh axis runs over, the one named last changes fastest.
Arguments:
- frames_in: bfloat16 [128, 32, 64, 512], P('tm', 'row'), may hold values from -6 to 6
- state_in: float32 [32, 64, 512], P('row'), may hold values from -12 to 12
- modulus: float32 [128, 256], replicated, may hold values from 0.05 to 1
- angle: float32 [256], replicated, may hold values from -3.140625 to 3.140625
- w_in: bfloat16 [3, 3, 512, 512], replicated, may hold values from -0.09375 to 0.09375
- w_out: bfloat16 [3, 3, 512, 512], replicated, may hold values from -0.0234375 to 0.0234375
Outputs:
- output: bfloat16 [128, 32, 64, 512], P('tm', 'row')
The draws below stay inside these ranges and needn't reach their ends.
All inputs are finite; a program needn't handle non-finite values.
Results may differ from the reference program's by a relative error of at most 0.005.
Values may be sent and summed in bfloat16 or wider, within the bound.
No kernel may reach another device: no remote copies, remote signals or barrier semaphores. Data moves between devices by JAX's collectives and lax.ppermute only.
A program may use at most 64 MiB of HBM per device.

```python
import jax
import jax.numpy as jnp
from jax import lax

C = 512
PAIRS = 256
W = 64
H = 32
SPAN_SNAPSHOTS = 128


def draw_modulus(key, part):
    gradual_seed, root_seed, quick_seed, multiplier_seed, spike_seed, layers_seed = jax.random.split(jax.random.fold_in(key, 7), 6)
    share = 0.5
    slow_pick = jax.random.uniform(gradual_seed, (PAIRS,), jnp.float32) < share
    slow_gap = jnp.exp(jax.random.uniform(root_seed, (PAIRS,), jnp.float32, jnp.log(0.001), jnp.log(0.01)))
    fast_rate = jax.random.uniform(quick_seed, (PAIRS,), jnp.float32, 0.6, 0.9)
    base_rate = jnp.where(slow_pick, 1.0 - slow_gap, fast_rate)
    factor = jnp.exp(jax.random.uniform(multiplier_seed, (SPAN_SNAPSHOTS, PAIRS), jnp.float32, -jnp.log(2.0), jnp.log(2.0)))
    damping_speeds = jnp.exp(jnp.log(base_rate)[None, :] * factor)
    spike_place = jax.random.randint(spike_seed, (3,), 0, SPAN_SNAPSHOTS)
    hidden_dimension = jax.random.uniform(layers_seed, (3, PAIRS), jnp.float32, 0.5, 0.8)
    snapshot_times = jnp.arange(SPAN_SNAPSHOTS)
    for spike_ordinal in range(3):
        spike_markers = (snapshot_times == spike_place[spike_ordinal])[:, None]
        damping_speeds = jnp.where(spike_markers, damping_speeds * hidden_dimension[spike_ordinal][None, :], damping_speeds)
    return damping_speeds.astype(jnp.float32)


def block_scale(key, extent, pieces, smallest, top_value):
    factor_of = 1.0
    for position, shards_of in pieces:
        steps = jax.random.uniform(jax.random.fold_in(jax.random.fold_in(key, 6), position), (shards_of,), jnp.float32, smallest / len(pieces), top_value / len(pieces))
        factor_of = factor_of * jnp.repeat(jnp.exp(steps), extent[position] // shards_of).reshape((-1,) + (1,) * (len(extent) - 1 - position))
    return factor_of


def noise(rng, extent, deviation, bound, shards=(), dtype=jnp.bfloat16):
    values = jax.random.normal(rng, extent, jnp.float32) * deviation
    if len(shards) > 0:
        values = block_scale(rng, extent, shards, -0.22, 0.18) * values
    return jnp.clip(values, min=-bound, max=bound).astype(dtype)


def setup_inputs(seed: int = 0) -> dict:
    key_list = jax.random.split(jax.random.key(seed), 7)
    frames_in = noise(key_list[0], (SPAN_SNAPSHOTS, H, W, C), 1.0, 6.0, ((0, 32), (1, 8)))
    state_in = noise(key_list[1], (H, W, C), 2.0, 12.0, ((0, 8),), jnp.float32)
    modulus = draw_modulus(jax.random.fold_in(key_list[6], 71), 0)
    angle = jnp.clip(jax.random.uniform(key_list[3], (PAIRS,), jnp.float32, -3.140625, 3.140625), -3.140625, 3.140625)
    w_in = noise(key_list[4], (3, 3, C, C), (9 * C) ** -0.5, 0.09375)
    w_out = noise(key_list[5], (3, 3, C, C), (144 * C) ** -0.5, 0.0234375)
    return {"frames_in": frames_in, "state_in": state_in, "modulus": modulus, "angle": angle, "w_in": w_in, "w_out": w_out}


def conv_frame(source, weight):
    padded = jnp.pad(source, ((1, 1), (1, 1), (0, 0)))
    height, columns, channels = source.shape
    summed = jnp.zeros((height * columns, weight.shape[3]), jnp.float32)
    for row_tap in range(3):
        for col_tap in range(3):
            window = padded[row_tap:row_tap + height, col_tap:col_tap + columns, :].reshape(-1, channels)
            summed = summed + jnp.dot(window, weight[row_tap, col_tap], preferred_element_type=jnp.float32)
    return summed.reshape(height, columns, -1)


def rotate(rate_re, rate_im, values):
    half = values.shape[-1] // 2
    part_re = values[..., :half]
    part_im = values[..., half:]
    return jnp.concatenate([rate_re * part_re - rate_im * part_im, rate_im * part_re + rate_re * part_im], axis=-1)


def reference(frames_in, state_in, modulus, angle, w_in, w_out):
    rate_re = modulus * jnp.cos(angle)[None, :]
    rate_im = modulus * jnp.sin(angle)[None, :]

    def advance(carried, inputs):
        one_frame, step_re, step_im = inputs
        update = conv_frame(one_frame, w_in)
        carried = rotate(step_re, step_im, carried) + update
        state_bf = carried.astype(jnp.bfloat16)
        result = jax.nn.gelu(conv_frame(state_bf, w_out), approximate=False).astype(jnp.bfloat16)
        return carried, result

    _, output = lax.scan(advance, state_in.astype(jnp.float32), (frames_in, rate_re, rate_im))
    return output
```

```python
import functools

import jax
import jax.numpy as jnp
from jax import lax
from jax.experimental import pallas as pl
from jax.experimental.pallas import tpu as pltpu
from jax.sharding import Mesh
from jax.sharding import PartitionSpec as P

TM = ("tm_0", "tm_1", "tm_2")
F32 = jnp.float32
BF16 = jnp.bfloat16
VM = pl.BlockSpec(memory_space=pltpu.VMEM)
HBM = pl.BlockSpec(memory_space=pl.ANY)

RATE, PROD, CORE, XPRE, XTOT, XIN, YPRE, YIN, ROWS = 0, 4, 8, 10, 13, 17, 18, 21, 22


def call(kernel, outs, specs, out_specs=None, scratch=(), flops=0, size=0, limit=24, aliases=None):
    return pl.pallas_call(
        kernel,
        out_shape=outs,
        in_specs=specs,
        out_specs=out_specs if out_specs is not None else jax.tree.map(lambda _: VM, outs),
        scratch_shapes=list(scratch),
        input_output_aliases=aliases or {},
        cost_estimate=pl.CostEstimate(flops=flops, bytes_accessed=size, transcendentals=0),
        compiler_params=pltpu.CompilerParams(vmem_limit_bytes=limit << 20),
    )


def cmul(a, b):
    return (a[0] * b[0] - a[1] * b[1], a[0] * b[1] + a[1] * b[0])


def powers(base, count):
    out = [(jnp.ones_like(base[0]), jnp.zeros_like(base[0]))]
    for _ in range(count):
        out.append(cmul(out[-1], base))
    return out


def prepare(frames, mod, ang, edge_first, edge_last, tab, sems, *, nx, ny, nf):
    rows = frames.shape[1]
    first = pltpu.make_async_copy(frames.at[:, 0], edge_first, sems.at[0])
    last = pltpu.make_async_copy(frames.at[:, rows - 1], edge_last, sems.at[1])
    first.start()
    last.start()
    y, x, c = (lax.axis_index(name) for name in TM)
    pairs = mod.shape[1]
    shape = (8, pairs)
    theta = jnp.broadcast_to(ang[...], shape)
    turn = (jnp.cos(theta), jnp.sin(theta))
    local = powers(turn, nf)
    chip_turn = powers(cmul(local[nf], local[nf]), nx)
    row_turn = powers(chip_turn[nx], ny)

    def put(index, size, angle):
        tab[index, :, :pairs] = size * angle[0]
        tab[index, :, pairs:] = size * angle[1]

    def product8(v):
        v = v * pltpu.roll(v, 7, 0)
        v = v * pltpu.roll(v, 6, 0)
        return v * pltpu.roll(v, 4, 0)

    def chip_rows(index):
        return mod[pl.ds(pl.multiple_of(index * 8, 8), 8), :]

    one = jnp.ones(shape, F32)
    zero = jnp.zeros(shape, F32)
    mine = chip_rows(y * nx + x)
    ms = [jnp.broadcast_to(mine[i : i + 1], shape) for i in range(2 * nf)]
    running = None
    for t in range(nf):
        m = jnp.where(c == 0, ms[t], ms[nf + t])
        running = m if running is None else running * m
        put(RATE + t, m, turn)
        put(PROD + t, running, local[t + 1])
    for core in range(2):
        total = ms[core * nf]
        for t in range(1, nf):
            total = total * ms[core * nf + t]
        put(CORE + core, total, local[nf])
    chips = [product8(chip_rows(y * nx + u)) for u in range(nx)]
    line = []
    for v in range(ny):
        total = product8(chip_rows(v * nx))
        for u in range(1, nx):
            total = total * product8(chip_rows(v * nx + u))
        line.append(total)

    def between(values, low, high):
        total = one
        for u, value in enumerate(values):
            total = total * jnp.where((u > low) & (u < high), value, one)
        return total

    for d in range(1, nx):
        put(XPRE + d - 1, jnp.where(x >= d, between(chips, x - d, x), zero), chip_turn[d - 1])
    for d in range(nx):
        source = lax.rem(x - d + nx, nx)
        angle = chip_turn[0]
        for k in range(nx):
            pick = source == nx - 1 - k
            angle = tuple(jnp.where(pick, new, old) for new, old in zip(chip_turn[k], angle))
        put(XTOT + d, between(chips, source, nx), angle)
    angle = chip_turn[0]
    for k in range(nx):
        angle = tuple(jnp.where(x == k, new, old) for new, old in zip(chip_turn[k], angle))
    put(XIN, between(chips, -1, x), angle)
    for d in range(1, ny):
        put(YPRE + d - 1, jnp.where(y >= d, between(line, y - d, y), zero), row_turn[d - 1])
    angle = row_turn[0]
    for k in range(ny):
        angle = tuple(jnp.where(y == k, new, old) for new, old in zip(row_turn[k], angle))
    put(YIN, between(line, -1, y), angle)
    first.wait()
    last.wait()


def mix_columns(left, middle, right, width):
    count = left.shape[0]
    column = lax.broadcasted_iota(jnp.int32, (count, 1), 0) % width
    left = jnp.where(column == 0, 0.0, pltpu.roll(left, 1, 0))
    right = jnp.where(column == width - 1, 0.0, pltpu.roll(right, count - 1, 0))
    return middle + left + right


def taps_of(inputs, weight, taps, width):
    lhs = jnp.concatenate(inputs, axis=1)
    parts = [
        jnp.dot(
            lhs,
            jnp.concatenate([weight[a, b] for a in taps], axis=0),
            preferred_element_type=F32,
        )
        for b in range(3)
    ]
    return mix_columns(*parts, width)


def flat(value):
    return value.reshape(value.shape[0] * value.shape[1], value.shape[2])


def conv_inside(x, w, acc):
    nf, rows, width, _ = x.shape
    for r in range(rows):
        taps = [a for a in range(3) if 0 <= r + a - 1 < rows]
        acc[r] = taps_of([flat(x[:, r + a - 1]) for a in taps], w, taps, width)


def turned(tab, index, value):
    pairs = value.shape[-1] // 2
    re, im = tab[index, :, :pairs], tab[index, :, pairs:]
    v_re, v_im = value[..., :pairs], value[..., pairs:]
    return jnp.concatenate([re * v_re - im * v_im, im * v_re + re * v_im], axis=-1)


def tiles(value):
    return value.astype(F32).reshape(-1, 8, value.shape[-1])


def finish_update(acc, low, high, w, tab, local, keep, send):
    nf, width, chans = low.shape
    rows = acc.shape[0]
    z, zs = lax.axis_index("row"), lax.axis_size("row")
    c = lax.axis_index(TM[2])
    first = taps_of([flat(low[...])], w, [0], width)
    last = taps_of([flat(high[...])], w, [2], width)
    first = acc[0] + jnp.where(z > 0, first, 0.0)
    last = acc[rows - 1] + jnp.where(z < zs - 1, last, 0.0)
    ends = [None] * rows
    for r in list(range(1, rows - 1)) + [0, rows - 1]:
        update = first if r == 0 else last if r == rows - 1 else acc[r]
        running = None
        for t in range(nf):
            new = tiles(update[t * width : (t + 1) * width])
            running = new if running is None else turned(tab, RATE + t, running) + new
            local[r, t] = running.reshape(width, chans)
        ends[r] = running.reshape(width, chans)
    half = rows // 2
    for i in range(half):
        keep[i] = jnp.where(c == 0, ends[i], ends[half + i])
        send[i] = jnp.where(c == 0, ends[half + i], ends[i])


def join_cores(keep, got, tab, chip, start):
    c = lax.axis_index(TM[2])
    for i in range(keep.shape[0]):
        early = jnp.where(c == 0, keep[i], got[i])
        late = jnp.where(c == 0, got[i], keep[i])
        start[i] = early
        total = turned(tab, CORE + 1, tiles(early)) + tiles(late)
        chip[i] = total.reshape(early.shape).astype(BF16)


def join_row(*refs):
    own, *got, tab, prefix, total = refs
    for i in range(own.shape[0]):
        shape = own.shape[1:]
        parts = [tiles(ref[i]) for ref in (own, *got)]
        before = whole = None
        for d, part in enumerate(parts):
            term = turned(tab, XTOT + d, part)
            whole = term if whole is None else whole + term
            if d > 0:
                term = turned(tab, XPRE + d - 1, part)
                before = term if before is None else before + term
        prefix[i] = before.reshape(shape)
        total[i] = whole.reshape(shape).astype(BF16)


def join_all(*refs):
    *got, prefix, start, state_in, tab, keep, send = refs
    c = lax.axis_index(TM[2])
    half = prefix.shape[0]
    for i in range(half):
        shape = prefix.shape[1:]
        entry = jnp.where(c == 0, state_in[i], state_in[half + i])
        total = turned(tab, YIN, tiles(entry))
        for d, ref in enumerate(got):
            total = total + turned(tab, YPRE + d, tiles(ref[i]))
        chip = turned(tab, XIN, total) + tiles(prefix[i])
        other = turned(tab, CORE, chip) + tiles(start[i])
        chip, other = chip.reshape(shape), other.reshape(shape)
        keep[i] = jnp.where(c == 0, chip, other)
        send[i] = jnp.where(c == 0, other, chip)


def make_state(local, keep, got, tab, top, middle, bottom):
    rows, nf, width, chans = local.shape
    c = lax.axis_index(TM[2])
    half = rows // 2
    for r in [0, rows - 1] + list(range(1, rows - 1)):
        mine = c == r // half
        entry = tiles(jnp.where(mine, keep[r % half], got[r % half]))
        for t in range(nf):
            state = tiles(local[r, t]) + turned(tab, PROD + t, entry)
            state = state.reshape(width, chans).astype(BF16)
            if r == 0:
                top[t] = state
            elif r == rows - 1:
                bottom[t] = state
            else:
                middle[r - 1, t] = state


def gelu(v):
    return 0.5 * v * (1.0 + lax.erf(v * (0.5**0.5)))


def conv_state(top, middle, bottom, w, acc_top, acc_bottom, out):
    nf, width, chans = top.shape
    rows = middle.shape[0] + 2

    def row(r):
        return flat(top[...] if r == 0 else bottom[...] if r == rows - 1 else middle[r - 1])

    for r in list(range(1, rows - 1)) + [0, rows - 1]:
        taps = [a for a in range(3) if 0 <= r + a - 1 < rows]
        result = taps_of([row(r + a - 1) for a in taps], w, taps, width)
        if r == 0:
            acc_top[...] = result
        elif r == rows - 1:
            acc_bottom[...] = result
        else:
            out[r - 1] = gelu(result).reshape(nf, width, chans).astype(BF16)


def finish_output(acc_top, acc_bottom, low, high, w, inside, out, edge, sems):
    nf, width, chans = low.shape
    rows = inside.shape[0] + 2
    z, zs = lax.axis_index("row"), lax.axis_size("row")
    copies = []
    for r in range(1, rows - 1):
        copies.append(pltpu.make_async_copy(inside.at[r - 1], out.at[:, r], sems.at[r]))
        copies[-1].start()
    for i, (acc, halo, tap, live, r) in enumerate(
        [(acc_top, low, 0, z > 0, 0), (acc_bottom, high, 2, z < zs - 1, rows - 1)]
    ):
        part = taps_of([flat(halo[...])], w, [tap], width)
        total = acc[...] + jnp.where(live, part, 0.0)
        edge[i] = gelu(total).reshape(nf, width, chans).astype(BF16)
        copies.append(pltpu.make_async_copy(edge.at[i], out.at[:, r], sems.at[r]))
        copies[-1].start()
    for copy in copies:
        copy.wait()


def ring(value, axis, distance):
    count = lax.axis_size(axis)
    return lax.ppermute(value, axis, [(i, (i + distance) % count) for i in range(count)])


def shards(frames, state_in, modulus, angle, w_in, w_out):
    nf, rows, width, chans = frames.shape
    ny, nx, _ = (lax.axis_size(name) for name in TM)
    half = rows // 2
    conv_flops = 2 * nf * rows * width * 9 * chans * chans
    conv_bytes = 9 * chans * chans * 2

    def shape(*dims, dtype=F32):
        return jax.ShapeDtypeStruct(dims, dtype)

    row_bf = shape(nf, width, chans, dtype=BF16)
    acc_row = shape(nf * width, chans)
    half_f32 = shape(half, width, chans)
    half_bf = shape(half, width, chans, dtype=BF16)

    first, last, tab = call(
        functools.partial(prepare, nx=nx, ny=ny, nf=nf),
        (row_bf, row_bf, shape(ROWS, 8, chans)),
        [HBM, VM, VM],
        scratch=[pltpu.SemaphoreType.DMA((2,))],
    )(frames, modulus, angle[None])
    low = ring(last, "row", 1)
    high = ring(first, "row", -1)
    acc = call(
        conv_inside,
        shape(rows, nf * width, chans),
        [VM, VM],
        flops=conv_flops * 10 // 12,
        size=conv_bytes,
    )(frames, w_in)
    local, keep, send = call(
        finish_update,
        (shape(rows, nf, width, chans), half_f32, half_f32),
        [VM] * 5,
        flops=conv_flops // 6,
        size=conv_bytes,
    )(acc, low, high, w_in, tab)
    got = ring(send, TM[2], 1)
    chip, start = call(join_cores, (half_bf, half_f32), [VM] * 3)(keep, got, tab)
    others = [ring(chip, TM[1], d) for d in range(1, nx)]
    prefix, total = call(join_row, (half_f32, half_bf), [VM] * (nx + 1))(chip, *others, tab)
    others = [ring(total, TM[0], d) for d in range(1, ny)]
    keep, send = call(join_all, (half_f32, half_f32), [VM] * (ny + 3))(
        *others, prefix, start, state_in, tab
    )
    got = ring(send, TM[2], 1)
    top, middle, bottom = call(
        make_state,
        (row_bf, shape(rows - 2, nf, width, chans, dtype=BF16), row_bf),
        [VM] * 4,
    )(local, keep, got, tab)
    low = ring(bottom, "row", 1)
    high = ring(top, "row", -1)
    acc_top, acc_bottom, inside = call(
        conv_state,
        (acc_row, acc_row, shape(rows - 2, nf, width, chans, dtype=BF16)),
        [VM] * 4,
        flops=conv_flops * 10 // 12,
        size=conv_bytes,
    )(top, middle, bottom, w_out)
    return call(
        finish_output,
        shape(nf, rows, width, chans, dtype=BF16),
        [VM] * 6,
        out_specs=HBM,
        scratch=[pltpu.VMEM((2, nf, width, chans), BF16), pltpu.SemaphoreType.DMA((rows,))],
        flops=conv_flops // 6,
        size=conv_bytes,
    )(acc_top, acc_bottom, low, high, w_out, inside)


def solution(mesh):
    chips = mesh.shape["tm"] // 2
    side = int(chips**0.5)
    finer = Mesh(
        mesh.devices.reshape(chips // side, side, 2, mesh.shape["row"]), (*TM, "row")
    )
    placed = (P(TM, "row", None, None), P("row", None, None), P(), P(), P(), P())
    return jax.shard_map(
        shards, mesh=finer, in_specs=placed, out_specs=P(TM, "row", None, None), check_vma=False
    )
```

```python
import functools

import jax
import jax.numpy as jnp
from jax import lax
from jax.experimental import pallas as pl
from jax.experimental.pallas import tpu as pltpu
from jax.sharding import Mesh
from jax.sharding import PartitionSpec as P

TM = ("tm_0", "tm_1", "tm_2")
F32 = jnp.float32
BF16 = jnp.bfloat16
VM = pl.BlockSpec(memory_space=pltpu.VMEM)
HBM = pl.BlockSpec(memory_space=pltpu.HBM)

RATE, PROD, CORE, XPRE, XTOT, XIN, YPRE, YIN, ROWS = 0, 4, 8, 10, 13, 17, 18, 21, 22


def call(kernel, outs, specs, out_specs=None, scratch=(), flops=0, size=0, limit=24, aliases=None):
    return pl.pallas_call(
        kernel,
        out_shape=outs,
        in_specs=specs,
        out_specs=out_specs if out_specs is not None else jax.tree.map(lambda _: VM, outs),
        scratch_shapes=list(scratch),
        input_output_aliases=aliases or {},
        cost_estimate=pl.CostEstimate(flops=flops, bytes_accessed=size, transcendentals=0),
        compiler_params=pltpu.CompilerParams(vmem_limit_bytes=limit << 20),
    )


def cmul(a, b):
    return (a[0] * b[0] - a[1] * b[1], a[0] * b[1] + a[1] * b[0])


def partners(index, count):
    if count == 2:
        return [1 - index]
    return [lax.rem(index + 2, 4), index + 1 - 2 * lax.rem(index, 2), 3 - index]


def powers(base, count):
    out = [(jnp.ones_like(base[0]), jnp.zeros_like(base[0]))]
    for _ in range(count):
        out.append(cmul(out[-1], base))
    return out


def edges(frames, first, last, sems):
    rows = frames.shape[1]
    copies = [
        pltpu.make_async_copy(frames.at[:, row], edge, sems.at[i])
        for i, (row, edge) in enumerate([(0, first), (rows - 1, last)])
    ]
    for copy in copies:
        copy.start()
    for copy in copies:
        copy.wait()


def fill_table(mod, ang, tab, nx, ny, nf):
    y, x, c = (lax.axis_index(name) for name in TM)
    pairs = mod.shape[1]
    shape = (8, pairs)
    theta = jnp.broadcast_to(ang[...], shape)
    turn = (jnp.cos(theta), jnp.sin(theta))
    local = powers(turn, nf)
    chip_turn = powers(cmul(local[nf], local[nf]), nx)
    row_turn = powers(chip_turn[nx], ny)

    def put(index, size, angle):
        tab[index, :, :pairs] = size * angle[0]
        tab[index, :, pairs:] = size * angle[1]

    def product8(v):
        v = v * pltpu.roll(v, 7, 0)
        v = v * pltpu.roll(v, 6, 0)
        return v * pltpu.roll(v, 4, 0)

    def chip_rows(index):
        return mod[pl.ds(pl.multiple_of(index * 8, 8), 8), :]

    one = jnp.ones(shape, F32)
    zero = jnp.zeros(shape, F32)
    mine = chip_rows(y * nx + x)
    ms = [jnp.broadcast_to(mine[i : i + 1], shape) for i in range(2 * nf)]
    running = None
    for t in range(nf):
        m = jnp.where(c == 0, ms[t], ms[nf + t])
        running = m if running is None else running * m
        put(RATE + t, m, turn)
        put(PROD + t, running, local[t + 1])
    for core in range(2):
        total = ms[core * nf]
        for t in range(1, nf):
            total = total * ms[core * nf + t]
        put(CORE + core, total, local[nf])
    chips = [product8(chip_rows(y * nx + u)) for u in range(nx)]
    line = []
    for v in range(ny):
        total = product8(chip_rows(v * nx))
        for u in range(1, nx):
            total = total * product8(chip_rows(v * nx + u))
        line.append(total)

    def between(values, low, high):
        total = one
        for u, value in enumerate(values):
            total = total * jnp.where((u > low) & (u < high), value, one)
        return total

    def turned_by(turns, count):
        angle = turns[0]
        for k in range(1, len(turns)):
            angle = tuple(jnp.where(count == k, new, old) for new, old in zip(turns[k], angle))
        return angle

    for i, p in enumerate(partners(x, nx)):
        size = jnp.where(p < x, between(chips, p, x), zero)
        put(XPRE + i, size, turned_by(chip_turn[:nx], x - 1 - p))
    for i, p in enumerate([x, *partners(x, nx)]):
        put(XTOT + i, between(chips, p, nx), turned_by(chip_turn[:nx], nx - 1 - p))
    put(XIN, between(chips, -1, x), turned_by(chip_turn[:nx], x))
    for i, p in enumerate(partners(y, ny)):
        size = jnp.where(p < y, between(line, p, y), zero)
        put(YPRE + i, size, turned_by(row_turn[:ny], y - 1 - p))
    put(YIN, between(line, -1, y), turned_by(row_turn[:ny], y))


def mix_columns(left, middle, right, width):
    count = left.shape[0]
    column = lax.broadcasted_iota(jnp.int32, (count, 1), 0) % width
    left = jnp.where(column == 0, 0.0, pltpu.roll(left, 1, 0))
    right = jnp.where(column == width - 1, 0.0, pltpu.roll(right, count - 1, 0))
    return middle + left + right


def taps_of(inputs, weight, taps, width):
    lhs = jnp.concatenate(inputs, axis=1)
    parts = [
        jnp.dot(
            lhs,
            jnp.concatenate([weight[a, b] for a in taps], axis=0),
            preferred_element_type=F32,
        )
        for b in range(3)
    ]
    return mix_columns(*parts, width)


def flat(value):
    return value.reshape(value.shape[0] * value.shape[1], value.shape[2])


def conv_inside(frames, w_far, mod_far, ang_far, acc, w, tab, x, mod, ang, x_sem, w_sem, m_sem, *, nx, ny):
    nf, rows, width, chans = frames.shape
    x_copies = [pltpu.make_async_copy(frames.at[:, r], x.at[r], x_sem.at[r]) for r in range(rows)]
    w_copies = [pltpu.make_async_copy(w_far.at[a], w.at[a], w_sem.at[a]) for a in range(3)]
    m_copies = [
        pltpu.make_async_copy(mod_far, mod, m_sem.at[0]),
        pltpu.make_async_copy(ang_far, ang, m_sem.at[1]),
    ]
    for copy in [*x_copies, w_copies[1], *m_copies, w_copies[0], w_copies[2]]:
        copy.start()
    for copy in x_copies:
        copy.wait()
    total = [[None] * rows for _ in range(3)]
    for a in (1, 0, 2):
        w_copies[a].wait()
        if a == 0:
            for copy in m_copies:
                copy.wait()
            fill_table(mod, ang, tab, nx, ny, nf)
        live = [r for r in range(rows) if 0 <= r + a - 1 < rows]
        lhs = flat(x[live[0] + a - 1 : live[-1] + a].reshape(len(live), nf * width, chans))
        for b in range(3):
            part = jnp.dot(lhs, w[a, b], preferred_element_type=F32)
            for i, r in enumerate(live):
                piece = part[i * nf * width : (i + 1) * nf * width]
                total[b][r] = piece if total[b][r] is None else total[b][r] + piece
    for r in range(rows):
        acc[r] = mix_columns(total[0][r], total[1][r], total[2][r], width)


def turned(tab, index, value):
    pairs = value.shape[-1] // 2
    re, im = tab[index, :, :pairs], tab[index, :, pairs:]
    v_re, v_im = value[..., :pairs], value[..., pairs:]
    return jnp.concatenate([re * v_re - im * v_im, im * v_re + re * v_im], axis=-1)


def tiles(value):
    return value.astype(F32).reshape(-1, 8, value.shape[-1])


def finish_update(acc, low, high, w, tab, local, keep, send, top, bottom):
    nf, width, chans = low.shape
    rows = acc.shape[0]
    z, zs = lax.axis_index("row"), lax.axis_size("row")
    c = lax.axis_index(TM[2])
    first = taps_of([flat(low[...])], w, [0], width)
    last = taps_of([flat(high[...])], w, [2], width)
    first = acc[0] + jnp.where(z > 0, first, 0.0)
    last = acc[rows - 1] + jnp.where(z < zs - 1, last, 0.0)
    ends = [None] * rows
    for r in list(range(1, rows - 1)) + [0, rows - 1]:
        update = first if r == 0 else last if r == rows - 1 else acc[r]
        running = None
        for t in range(nf):
            new = tiles(update[t * width : (t + 1) * width])
            running = new if running is None else turned(tab, RATE + t, running) + new
            local[r, t] = running.reshape(width, chans)
            if r == 0:
                top[t] = local[r, t].astype(BF16)
            elif r == rows - 1:
                bottom[t] = local[r, t].astype(BF16)
        ends[r] = running.reshape(width, chans)
    half = rows // 2
    for i in range(half):
        keep[i] = jnp.where(c == 0, ends[i], ends[half + i])
        send[i] = jnp.where(c == 0, ends[half + i], ends[i])


def join_cores(keep, got, tab, chip, start):
    c = lax.axis_index(TM[2])
    for i in range(keep.shape[0]):
        early = jnp.where(c == 0, keep[i], got[i])
        late = jnp.where(c == 0, got[i], keep[i])
        start[i] = early
        total = turned(tab, CORE + 1, tiles(early)) + tiles(late)
        chip[i] = total.reshape(early.shape).astype(BF16)


def join_row(*refs):
    own, *got, tab, prefix, total = refs
    for i in range(own.shape[0]):
        shape = own.shape[1:]
        parts = [tiles(ref[i]) for ref in (own, *got)]
        before = whole = None
        for d, part in enumerate(parts):
            term = turned(tab, XTOT + d, part)
            whole = term if whole is None else whole + term
            if d > 0:
                term = turned(tab, XPRE + d - 1, part)
                before = term if before is None else before + term
        prefix[i] = before.reshape(shape)
        total[i] = whole.reshape(shape).astype(BF16)


def join_all(*refs):
    *got, prefix, start, state_in, tab, keep, send, edge_keep, edge_send = refs
    c = lax.axis_index(TM[2])
    half = prefix.shape[0]
    for i in range(half):
        shape = prefix.shape[1:]
        entry = jnp.where(c == 0, state_in[i], state_in[half + i])
        total = turned(tab, YIN, tiles(entry))
        for d, ref in enumerate(got):
            total = total + turned(tab, YPRE + d, tiles(ref[i]))
        chip = turned(tab, XIN, total) + tiles(prefix[i])
        other = turned(tab, CORE, chip) + tiles(start[i])
        chip, other = chip.reshape(shape), other.reshape(shape)
        keep[i] = jnp.where(c == 0, chip, other)
        send[i] = jnp.where(c == 0, other, chip)
    edge_keep[...] = jnp.where(c == 0, keep[0], keep[half - 1])
    edge_send[...] = jnp.where(c == 0, send[0], send[half - 1])


def states(local, entry, tab):
    nf, width, chans = local.shape
    entry = tiles(entry)
    return jnp.concatenate(
        [
            (tiles(local[t]) + turned(tab, PROD + t, entry)).reshape(width, chans).astype(BF16)
            for t in range(nf)
        ],
        axis=0,
    )


def gelu(v):
    return 0.5 * v * (1.0 + lax.erf(v * (0.5**0.5)))


def conv_state(local, keep, got, tab, w, acc_top, acc_bottom, out):
    rows, nf, width, chans = local.shape
    c = lax.axis_index(TM[2])
    half = rows // 2
    row = []
    for r in range(rows):
        entry = jnp.where(c == r // half, keep[r % half], got[r % half])
        row.append(states(local[r], entry, tab))
    for r in list(range(1, rows - 1)) + [0, rows - 1]:
        taps = [a for a in range(3) if 0 <= r + a - 1 < rows]
        result = taps_of([row[r + a - 1] for a in taps], w, taps, width)
        if r == 0:
            acc_top[...] = result
        elif r == rows - 1:
            acc_bottom[...] = result
        else:
            out[r - 1] = gelu(result).reshape(nf, width, chans).astype(BF16)


def finish_output(
    acc_top, acc_bottom, low, high, same, cross, tab, w, inside, out, edge, sems
):
    nf, width, chans = low.shape
    rows = inside.shape[0] + 2
    z, zs = lax.axis_index("row"), lax.axis_size("row")
    c = lax.axis_index(TM[2])
    copies = []
    for r in range(1, rows - 1):
        copies.append(pltpu.make_async_copy(inside.at[r - 1], out.at[:, r], sems.at[r]))
        copies[-1].start()
    for i, (acc, halo, entry, tap, live, r) in enumerate(
        [
            (acc_top, low, jnp.where(c == 0, cross[...], same[...]), 0, z > 0, 0),
            (acc_bottom, high, jnp.where(c == 0, same[...], cross[...]), 2, z < zs - 1, rows - 1),
        ]
    ):
        part = taps_of([states(halo[...], entry, tab)], w, [tap], width)
        total = acc[...] + jnp.where(live, part, 0.0)
        edge[i] = gelu(total).reshape(nf, width, chans).astype(BF16)
        copies.append(pltpu.make_async_copy(edge.at[i], out.at[:, r], sems.at[r]))
        copies[-1].start()
    for copy in copies:
        copy.wait()


def ring(value, axis, distance):
    count = lax.axis_size(axis)
    return lax.ppermute(value, axis, [(i, (i + distance) % count) for i in range(count)])


def others(value, axis):
    count = lax.axis_size(axis)
    pairs = [[(i, p) for i, p in enumerate(group)] for group in zip(*(
        [int(p) for p in host_partners(i, count)] for i in range(count)
    ))]
    return [lax.ppermute(value, axis, pair) for pair in pairs]


def host_partners(index, count):
    if count == 2:
        return [1 - index]
    return [(index + 2) % 4, index ^ 1, 3 - index]


def shards(frames, state_in, modulus, angle, w_in, w_out):
    nf, rows, width, chans = frames.shape
    ny, nx, _ = (lax.axis_size(name) for name in TM)
    zs = lax.axis_size("row")
    half = rows // 2
    conv_flops = 2 * nf * rows * width * 9 * chans * chans
    conv_bytes = 9 * chans * chans * 2

    def shape(*dims, dtype=F32):
        return jax.ShapeDtypeStruct(dims, dtype)

    row_bf = shape(nf, width, chans, dtype=BF16)
    acc_row = shape(nf * width, chans)
    half_f32 = shape(half, width, chans)
    half_bf = shape(half, width, chans, dtype=BF16)
    one_row = shape(width, chans)

    first, last = call(edges, (row_bf, row_bf), [HBM], scratch=[pltpu.SemaphoreType.DMA((2,))])(
        frames
    )
    low = ring(last, "row", 1)
    high = ring(first, "row", -1)
    acc, w_near, tab = call(
        functools.partial(conv_inside, nx=nx, ny=ny),
        (
            shape(rows, nf * width, chans),
            shape(*w_in.shape, dtype=BF16),
            shape(ROWS, 8, chans),
        ),
        [HBM] * 4,
        scratch=[
            pltpu.VMEM((rows, nf, width, chans), BF16),
            pltpu.VMEM(modulus.shape, F32),
            pltpu.VMEM((1, angle.shape[0]), F32),
            pltpu.SemaphoreType.DMA((rows,)),
            pltpu.SemaphoreType.DMA((3,)),
            pltpu.SemaphoreType.DMA((2,)),
        ],
        flops=conv_flops * 10 // 12,
        size=conv_bytes,
    )(frames, w_in, modulus, angle[None])
    local, keep, send, top, bottom = call(
        finish_update,
        (shape(rows, nf, width, chans), half_f32, half_f32, row_bf, row_bf),
        [VM] * 5,
        flops=conv_flops // 6,
        size=conv_bytes,
    )(acc, low, high, w_near, tab)
    got = ring(send, TM[2], 1)
    low = ring(bottom, "row", 1)
    high = ring(top, "row", -1)
    chip, start = call(join_cores, (half_bf, half_f32), [VM] * 3)(keep, got, tab)
    prefix, total = call(join_row, (half_f32, half_bf), [VM] * (nx + 1))(
        chip, *others(chip, TM[1]), tab
    )
    keep, send, edge_keep, edge_send = call(
        join_all, (half_f32, half_f32, one_row, one_row), [VM] * (ny + 3)
    )(*others(total, TM[0]), prefix, start, state_in, tab)
    got = ring(send, TM[2], 1)
    step = [-1, 1]
    same, cross = (
        lax.ppermute(
            value,
            (TM[2], "row"),
            [
                (c * zs + z, (c ^ flip) * zs + (z + step[c]) % zs)
                for c in range(2)
                for z in range(zs)
            ],
        )
        for value, flip in ((edge_keep, 0), (edge_send, 1))
    )
    acc_top, acc_bottom, inside = call(
        conv_state,
        (acc_row, acc_row, shape(rows - 2, nf, width, chans, dtype=BF16)),
        [VM] * 5,
        flops=conv_flops * 10 // 12,
        size=conv_bytes,
    )(local, keep, got, tab, w_out)
    return call(
        finish_output,
        shape(nf, rows, width, chans, dtype=BF16),
        [VM] * 9,
        out_specs=HBM,
        scratch=[pltpu.VMEM((2, nf, width, chans), BF16), pltpu.SemaphoreType.DMA((rows,))],
        flops=conv_flops // 6,
        size=conv_bytes,
    )(acc_top, acc_bottom, low, high, same, cross, tab, w_out, inside)


def solution(mesh):
    chips = mesh.shape["tm"] // 2
    side = int(chips**0.5)
    finer = Mesh(
        mesh.devices.reshape(chips // side, side, 2, mesh.shape["row"]), (*TM, "row")
    )
    placed = (P(TM, "row", None, None), P("row", None, None), P(), P(), P(), P())
    return jax.shard_map(
        shards, mesh=finer, in_specs=placed, out_specs=P(TM, "row", None, None), check_vma=False
    )
```

```python
import functools

import jax
import jax.numpy as jnp
from jax import lax
from jax.experimental import pallas as pl
from jax.experimental.pallas import tpu as pltpu
from jax.sharding import Mesh
from jax.sharding import PartitionSpec as P

TM = ("tm_0", "tm_1", "tm_2")
F32 = jnp.float32
BF16 = jnp.bfloat16
VM = pl.BlockSpec(memory_space=pltpu.VMEM)
HBM = pl.BlockSpec(memory_space=pltpu.HBM)

RATE, PROD, CORE, XPRE, XTOT, XIN, YPRE, YIN, ROWS = 0, 4, 8, 10, 13, 17, 18, 21, 22


def call(kernel, outs, specs, out_specs=None, scratch=(), flops=0, size=0, limit=24, aliases=None):
    return pl.pallas_call(
        kernel,
        out_shape=outs,
        in_specs=specs,
        out_specs=out_specs if out_specs is not None else jax.tree.map(lambda _: VM, outs),
        scratch_shapes=list(scratch),
        input_output_aliases=aliases or {},
        cost_estimate=pl.CostEstimate(flops=flops, bytes_accessed=size, transcendentals=0),
        compiler_params=pltpu.CompilerParams(vmem_limit_bytes=limit << 20),
    )


def cmul(a, b):
    return (a[0] * b[0] - a[1] * b[1], a[0] * b[1] + a[1] * b[0])


def partners(index, count):
    if count == 2:
        return [1 - index]
    return [3 - index, index + 1 - 2 * lax.rem(index, 2), lax.rem(index + 2, 4)]


def powers(base, count):
    out = [(jnp.ones_like(base[0]), jnp.zeros_like(base[0]))]
    for _ in range(count):
        out.append(cmul(out[-1], base))
    return out


def edges(frames, first, last, sems):
    rows = frames.shape[1]
    copies = [
        pltpu.make_async_copy(frames.at[:, row], edge, sems.at[i])
        for i, (row, edge) in enumerate([(0, first), (rows - 1, last)])
    ]
    for copy in copies:
        copy.start()
    for copy in copies:
        copy.wait()


def fill_table(mod, ang, tab, nx, ny, nf):
    y, x, c = (lax.axis_index(name) for name in TM)
    pairs = mod.shape[1]
    shape = (8, pairs)
    theta = jnp.broadcast_to(ang[...], shape)
    turn = (jnp.cos(theta), jnp.sin(theta))
    local = powers(turn, nf)
    chip_turn = powers(cmul(local[nf], local[nf]), nx)
    row_turn = powers(chip_turn[nx], ny)

    def put(index, size, angle):
        tab[index, :, :pairs] = size * angle[0]
        tab[index, :, pairs:] = size * angle[1]

    def product8(v):
        v = v * pltpu.roll(v, 7, 0)
        v = v * pltpu.roll(v, 6, 0)
        return v * pltpu.roll(v, 4, 0)

    def chip_rows(index):
        return mod[pl.ds(pl.multiple_of(index * 8, 8), 8), :]

    one = jnp.ones(shape, F32)
    zero = jnp.zeros(shape, F32)
    mine = chip_rows(y * nx + x)
    ms = [jnp.broadcast_to(mine[i : i + 1], shape) for i in range(2 * nf)]
    running = None
    for t in range(nf):
        m = jnp.where(c == 0, ms[t], ms[nf + t])
        running = m if running is None else running * m
        put(RATE + t, m, turn)
        put(PROD + t, running, local[t + 1])
    for core in range(2):
        total = ms[core * nf]
        for t in range(1, nf):
            total = total * ms[core * nf + t]
        put(CORE + core, total, local[nf])
    chips = [product8(chip_rows(y * nx + u)) for u in range(nx)]
    line = []
    for v in range(ny):
        total = product8(chip_rows(v * nx))
        for u in range(1, nx):
            total = total * product8(chip_rows(v * nx + u))
        line.append(total)

    def between(values, low, high):
        total = one
        for u, value in enumerate(values):
            total = total * jnp.where((u > low) & (u < high), value, one)
        return total

    def turned_by(turns, count):
        angle = turns[0]
        for k in range(1, len(turns)):
            angle = tuple(jnp.where(count == k, new, old) for new, old in zip(turns[k], angle))
        return angle

    for i, p in enumerate(partners(x, nx)):
        size = jnp.where(p < x, between(chips, p, x), zero)
        put(XPRE + i, size, turned_by(chip_turn[:nx], x - 1 - p))
    for i, p in enumerate([x, *partners(x, nx)]):
        put(XTOT + i, between(chips, p, nx), turned_by(chip_turn[:nx], nx - 1 - p))
    put(XIN, between(chips, -1, x), turned_by(chip_turn[:nx], x))
    for i, p in enumerate(partners(y, ny)):
        size = jnp.where(p < y, between(line, p, y), zero)
        put(YPRE + i, size, turned_by(row_turn[:ny], y - 1 - p))
    put(YIN, between(line, -1, y), turned_by(row_turn[:ny], y))


def mix_columns(left, middle, right, width):
    count = left.shape[0]
    column = lax.broadcasted_iota(jnp.int32, (count, 1), 0) % width
    left = jnp.where(column == 0, 0.0, pltpu.roll(left, 1, 0))
    right = jnp.where(column == width - 1, 0.0, pltpu.roll(right, count - 1, 0))
    return middle + left + right


def taps_of(inputs, weight, taps, width):
    lhs = jnp.concatenate(inputs, axis=1)
    parts = [
        jnp.dot(
            lhs,
            jnp.concatenate([weight[a, b] for a in taps], axis=0),
            preferred_element_type=F32,
        )
        for b in range(3)
    ]
    return mix_columns(*parts, width)


def flat(value):
    return value.reshape(value.shape[0] * value.shape[1], value.shape[2])


def conv_inside(frames, w_far, mod_far, ang_far, acc, w, tab, x, mod, ang, x_sem, w_sem, m_sem, *, nx, ny):
    nf, rows, width, chans = frames.shape
    x_copies = [pltpu.make_async_copy(frames.at[:, r], x.at[r], x_sem.at[r]) for r in range(rows)]
    w_copies = [pltpu.make_async_copy(w_far.at[a], w.at[a], w_sem.at[a]) for a in range(3)]
    m_copies = [
        pltpu.make_async_copy(mod_far, mod, m_sem.at[0]),
        pltpu.make_async_copy(ang_far, ang, m_sem.at[1]),
    ]
    for copy in [*x_copies, w_copies[1], *m_copies, w_copies[0], w_copies[2]]:
        copy.start()
    for copy in x_copies:
        copy.wait()
    total = [[None] * rows for _ in range(3)]
    for a in (1, 0, 2):
        w_copies[a].wait()
        if a == 0:
            for copy in m_copies:
                copy.wait()
            fill_table(mod, ang, tab, nx, ny, nf)
        live = [r for r in range(rows) if 0 <= r + a - 1 < rows]
        lhs = flat(x[live[0] + a - 1 : live[-1] + a].reshape(len(live), nf * width, chans))
        for b in range(3):
            part = jnp.dot(lhs, w[a, b], preferred_element_type=F32)
            for i, r in enumerate(live):
                piece = part[i * nf * width : (i + 1) * nf * width]
                total[b][r] = piece if total[b][r] is None else total[b][r] + piece
    for r in range(rows):
        acc[r] = mix_columns(total[0][r], total[1][r], total[2][r], width)


def turned(tab, index, value):
    pairs = value.shape[-1] // 2
    re, im = tab[index, :, :pairs], tab[index, :, pairs:]
    v_re, v_im = value[..., :pairs], value[..., pairs:]
    return jnp.concatenate([re * v_re - im * v_im, im * v_re + re * v_im], axis=-1)


def tiles(value):
    return value.astype(F32).reshape(-1, 8, value.shape[-1])


def finish_update(acc, low, high, w, tab, local, keep, send, top, bottom):
    nf, width, chans = low.shape
    rows = acc.shape[0]
    z, zs = lax.axis_index("row"), lax.axis_size("row")
    c = lax.axis_index(TM[2])
    first = taps_of([flat(low[...])], w, [0], width)
    last = taps_of([flat(high[...])], w, [2], width)
    first = acc[0] + jnp.where(z > 0, first, 0.0)
    last = acc[rows - 1] + jnp.where(z < zs - 1, last, 0.0)
    ends = [None] * rows
    for r in list(range(1, rows - 1)) + [0, rows - 1]:
        update = first if r == 0 else last if r == rows - 1 else acc[r]
        running = None
        for t in range(nf):
            new = tiles(update[t * width : (t + 1) * width])
            running = new if running is None else turned(tab, RATE + t, running) + new
            local[r, t] = running.reshape(width, chans)
            if r == 0:
                top[t] = local[r, t].astype(BF16)
            elif r == rows - 1:
                bottom[t] = local[r, t].astype(BF16)
        ends[r] = running.reshape(width, chans)
    half = rows // 2
    for i in range(half):
        keep[i] = jnp.where(c == 0, ends[i], ends[half + i])
        send[i] = jnp.where(c == 0, ends[half + i], ends[i])


def join_cores(keep, got, tab, chip, start):
    c = lax.axis_index(TM[2])
    for i in range(keep.shape[0]):
        early = jnp.where(c == 0, keep[i], got[i])
        late = jnp.where(c == 0, got[i], keep[i])
        start[i] = early
        total = turned(tab, CORE + 1, tiles(early)) + tiles(late)
        chip[i] = total.reshape(early.shape).astype(BF16)


def join_row(*refs):
    own, *got, tab, prefix, total = refs
    for i in range(own.shape[0]):
        shape = own.shape[1:]
        parts = [tiles(ref[i]) for ref in (own, *got)]
        before = whole = None
        for d, part in enumerate(parts):
            term = turned(tab, XTOT + d, part)
            whole = term if whole is None else whole + term
            if d > 0:
                term = turned(tab, XPRE + d - 1, part)
                before = term if before is None else before + term
        prefix[i] = before.reshape(shape)
        total[i] = whole.reshape(shape).astype(BF16)


def join_all(*refs):
    *got, prefix, start, state_in, tab, keep, send, edge_keep, edge_send = refs
    c = lax.axis_index(TM[2])
    half = prefix.shape[0]
    for i in range(half):
        shape = prefix.shape[1:]
        entry = jnp.where(c == 0, state_in[i], state_in[half + i])
        total = turned(tab, YIN, tiles(entry))
        for d, ref in enumerate(got):
            total = total + turned(tab, YPRE + d, tiles(ref[i]))
        chip = turned(tab, XIN, total) + tiles(prefix[i])
        other = turned(tab, CORE, chip) + tiles(start[i])
        chip, other = chip.reshape(shape), other.reshape(shape)
        keep[i] = jnp.where(c == 0, chip, other)
        send[i] = jnp.where(c == 0, other, chip)
    edge_keep[...] = jnp.where(c == 0, keep[0], keep[half - 1])
    edge_send[...] = jnp.where(c == 0, send[0], send[half - 1])


def states(local, entry, tab):
    nf, width, chans = local.shape
    entry = tiles(entry)
    return jnp.concatenate(
        [
            (tiles(local[t]) + turned(tab, PROD + t, entry)).reshape(width, chans).astype(BF16)
            for t in range(nf)
        ],
        axis=0,
    )


def gelu(v):
    return 0.5 * v * (1.0 + lax.erf(v * (0.5**0.5)))


def conv_state(local, keep, got, tab, w, acc_top, acc_bottom, out):
    rows, nf, width, chans = local.shape
    c = lax.axis_index(TM[2])
    half = rows // 2
    row = []
    for r in range(rows):
        entry = jnp.where(c == r // half, keep[r % half], got[r % half])
        row.append(states(local[r], entry, tab))
    for r in list(range(1, rows - 1)) + [0, rows - 1]:
        taps = [a for a in range(3) if 0 <= r + a - 1 < rows]
        result = taps_of([row[r + a - 1] for a in taps], w, taps, width)
        if r == 0:
            acc_top[...] = result
        elif r == rows - 1:
            acc_bottom[...] = result
        else:
            out[r - 1] = gelu(result).reshape(nf, width, chans).astype(BF16)


def finish_output(
    acc_top, acc_bottom, low, high, same, cross, tab, w, inside, out, edge, sems
):
    nf, width, chans = low.shape
    rows = inside.shape[0] + 2
    z, zs = lax.axis_index("row"), lax.axis_size("row")
    c = lax.axis_index(TM[2])
    copies = []
    for r in range(1, rows - 1):
        copies.append(pltpu.make_async_copy(inside.at[r - 1], out.at[:, r], sems.at[r]))
        copies[-1].start()
    for i, (acc, halo, entry, tap, live, r) in enumerate(
        [
            (acc_top, low, jnp.where(c == 0, cross[...], same[...]), 0, z > 0, 0),
            (acc_bottom, high, jnp.where(c == 0, same[...], cross[...]), 2, z < zs - 1, rows - 1),
        ]
    ):
        part = taps_of([states(halo[...], entry, tab)], w, [tap], width)
        total = acc[...] + jnp.where(live, part, 0.0)
        edge[i] = gelu(total).reshape(nf, width, chans).astype(BF16)
        copies.append(pltpu.make_async_copy(edge.at[i], out.at[:, r], sems.at[r]))
        copies[-1].start()
    for copy in copies:
        copy.wait()


def ring(value, axis, distance):
    count = lax.axis_size(axis)
    return lax.ppermute(value, axis, [(i, (i + distance) % count) for i in range(count)])


def others(value, axis):
    count = lax.axis_size(axis)
    pairs = [[(i, p) for i, p in enumerate(group)] for group in zip(*(
        [int(p) for p in host_partners(i, count)] for i in range(count)
    ))]
    return [lax.ppermute(value, axis, pair) for pair in pairs]


def host_partners(index, count):
    if count == 2:
        return [1 - index]
    return [3 - index, index ^ 1, (index + 2) % 4]


def shards(frames, state_in, modulus, angle, w_in, w_out):
    nf, rows, width, chans = frames.shape
    ny, nx, _ = (lax.axis_size(name) for name in TM)
    zs = lax.axis_size("row")
    half = rows // 2
    frames, modulus, w_in = (
        pltpu.with_memory_space_constraint(v, pltpu.HBM) for v in (frames, modulus, w_in)
    )
    angle = pltpu.with_memory_space_constraint(angle[None], pltpu.HBM)
    conv_flops = 2 * nf * rows * width * 9 * chans * chans
    conv_bytes = 9 * chans * chans * 2

    def shape(*dims, dtype=F32):
        return jax.ShapeDtypeStruct(dims, dtype)

    row_bf = shape(nf, width, chans, dtype=BF16)
    acc_row = shape(nf * width, chans)
    half_f32 = shape(half, width, chans)
    half_bf = shape(half, width, chans, dtype=BF16)
    one_row = shape(width, chans)

    first, last = call(edges, (row_bf, row_bf), [HBM], scratch=[pltpu.SemaphoreType.DMA((2,))])(
        frames
    )
    low = ring(last, "row", 1)
    high = ring(first, "row", -1)
    acc, w_near, tab = call(
        functools.partial(conv_inside, nx=nx, ny=ny),
        (
            shape(rows, nf * width, chans),
            shape(*w_in.shape, dtype=BF16),
            shape(ROWS, 8, chans),
        ),
        [HBM] * 4,
        scratch=[
            pltpu.VMEM((rows, nf, width, chans), BF16),
            pltpu.VMEM(modulus.shape, F32),
            pltpu.VMEM(angle.shape, F32),
            pltpu.SemaphoreType.DMA((rows,)),
            pltpu.SemaphoreType.DMA((3,)),
            pltpu.SemaphoreType.DMA((2,)),
        ],
        flops=conv_flops * 10 // 12,
        size=conv_bytes,
    )(frames, w_in, modulus, angle)
    local, keep, send, top, bottom = call(
        finish_update,
        (shape(rows, nf, width, chans), half_f32, half_f32, row_bf, row_bf),
        [VM] * 5,
        flops=conv_flops // 6,
        size=conv_bytes,
    )(acc, low, high, w_near, tab)
    got = ring(send, TM[2], 1)
    low = ring(bottom, "row", 1)
    high = ring(top, "row", -1)
    chip, start = call(join_cores, (half_bf, half_f32), [VM] * 3)(keep, got, tab)
    across = others(chip, TM[1])
    prefix, total = call(join_row, (half_f32, half_bf), [VM] * (nx + 1))(
        chip, *across, tab
    )
    keep, send, edge_keep, edge_send = call(
        join_all, (half_f32, half_f32, one_row, one_row), [VM] * (ny + 3)
    )(*others(total, TM[0]), prefix, start, state_in, tab)
    got = ring(send, TM[2], 1)
    step = [-1, 1]
    same, cross = (
        lax.ppermute(
            value,
            (TM[2], "row"),
            [
                (c * zs + z, (c ^ flip) * zs + (z + step[c]) % zs)
                for c in range(2)
                for z in range(zs)
            ],
        )
        for value, flip in ((edge_keep, 0), (edge_send, 1))
    )
    acc_top, acc_bottom, inside = call(
        conv_state,
        (acc_row, acc_row, shape(rows - 2, nf, width, chans, dtype=BF16)),
        [VM] * 5,
        flops=conv_flops * 10 // 12,
        size=conv_bytes,
    )(local, keep, got, tab, w_out)
    return call(
        finish_output,
        shape(nf, rows, width, chans, dtype=BF16),
        [VM] * 9,
        out_specs=HBM,
        scratch=[pltpu.VMEM((2, nf, width, chans), BF16), pltpu.SemaphoreType.DMA((rows,))],
        flops=conv_flops // 6,
        size=conv_bytes,
    )(acc_top, acc_bottom, low, high, same, cross, tab, w_out, inside)


def solution(mesh):
    chips = mesh.shape["tm"] // 2
    side = int(chips**0.5)
    finer = Mesh(
        mesh.devices.reshape(chips // side, side, 2, mesh.shape["row"]), (*TM, "row")
    )
    placed = (P(TM, "row", None, None), P("row", None, None), P(), P(), P(), P())

    return jax.shard_map(
        shards, mesh=finer, in_specs=placed, out_specs=P(TM, "row", None, None), check_vma=False
    )
```

```python
import functools

import jax
import jax.numpy as jnp
from jax import lax
from jax.experimental import pallas as pl
from jax.experimental.pallas import tpu as pltpu
from jax.sharding import Mesh
from jax.sharding import PartitionSpec as P

TM = ("tm_0", "tm_1", "tm_2")
F32 = jnp.float32
BF16 = jnp.bfloat16
VM = pl.BlockSpec(memory_space=pltpu.VMEM)
HBM = pl.BlockSpec(memory_space=pltpu.HBM)

RATE, PROD, CORE, XPRE, XTOT, XIN, YPRE, YIN, ROWS = 0, 4, 8, 10, 13, 17, 18, 21, 22


def call(kernel, outs, specs, out_specs=None, scratch=(), flops=0, size=0, limit=24, aliases=None):
    return pl.pallas_call(
        kernel,
        out_shape=outs,
        in_specs=specs,
        out_specs=out_specs if out_specs is not None else jax.tree.map(lambda _: VM, outs),
        scratch_shapes=list(scratch),
        input_output_aliases=aliases or {},
        cost_estimate=pl.CostEstimate(flops=flops, bytes_accessed=size, transcendentals=0),
        compiler_params=pltpu.CompilerParams(vmem_limit_bytes=limit << 20),
    )


def cmul(a, b):
    return (a[0] * b[0] - a[1] * b[1], a[0] * b[1] + a[1] * b[0])


def partners(index, count):
    if count == 2:
        return [1 - index]
    return [3 - index, index + 1 - 2 * lax.rem(index, 2), lax.rem(index + 2, 4)]


def powers(base, count):
    out = [(jnp.ones_like(base[0]), jnp.zeros_like(base[0]))]
    for _ in range(count):
        out.append(cmul(out[-1], base))
    return out


def edges(frames, first, last, sems):
    rows = frames.shape[1]
    copies = [
        pltpu.make_async_copy(frames.at[:, row], edge, sems.at[i])
        for i, (row, edge) in enumerate([(0, first), (rows - 1, last)])
    ]
    for copy in copies:
        copy.start()
    for copy in copies:
        copy.wait()


def fill_table(mod, ang, tab, nx, ny, nf):
    y, x, c = (lax.axis_index(name) for name in TM)
    pairs = mod.shape[1]
    shape = (8, pairs)
    theta = jnp.broadcast_to(ang[...], shape)
    turn = (jnp.cos(theta), jnp.sin(theta))
    local = powers(turn, nf)
    chip_turn = powers(cmul(local[nf], local[nf]), nx)
    row_turn = powers(chip_turn[nx], ny)

    def put(index, size, angle):
        tab[index, :, :pairs] = size * angle[0]
        tab[index, :, pairs:] = size * angle[1]

    def product8(v):
        v = v * pltpu.roll(v, 7, 0)
        v = v * pltpu.roll(v, 6, 0)
        return v * pltpu.roll(v, 4, 0)

    def chip_rows(index):
        return mod[pl.ds(pl.multiple_of(index * 8, 8), 8), :]

    one = jnp.ones(shape, F32)
    zero = jnp.zeros(shape, F32)
    mine = chip_rows(y * nx + x)
    ms = [jnp.broadcast_to(mine[i : i + 1], shape) for i in range(2 * nf)]
    running = None
    for t in range(nf):
        m = jnp.where(c == 0, ms[t], ms[nf + t])
        running = m if running is None else running * m
        put(RATE + t, m, turn)
        put(PROD + t, running, local[t + 1])
    for core in range(2):
        total = ms[core * nf]
        for t in range(1, nf):
            total = total * ms[core * nf + t]
        put(CORE + core, total, local[nf])
    chips = [product8(chip_rows(y * nx + u)) for u in range(nx)]
    line = []
    for v in range(ny):
        total = product8(chip_rows(v * nx))
        for u in range(1, nx):
            total = total * product8(chip_rows(v * nx + u))
        line.append(total)

    def between(values, low, high):
        total = one
        for u, value in enumerate(values):
            total = total * jnp.where((u > low) & (u < high), value, one)
        return total

    def turned_by(turns, count):
        angle = turns[0]
        for k in range(1, len(turns)):
            angle = tuple(jnp.where(count == k, new, old) for new, old in zip(turns[k], angle))
        return angle

    for i, p in enumerate(partners(x, nx)):
        size = jnp.where(p < x, between(chips, p, x), zero)
        put(XPRE + i, size, turned_by(chip_turn[:nx], x - 1 - p))
    for i, p in enumerate([x, *partners(x, nx)]):
        put(XTOT + i, between(chips, p, nx), turned_by(chip_turn[:nx], nx - 1 - p))
    put(XIN, between(chips, -1, x), turned_by(chip_turn[:nx], x))
    for i, p in enumerate(partners(y, ny)):
        size = jnp.where(p < y, between(line, p, y), zero)
        put(YPRE + i, size, turned_by(row_turn[:ny], y - 1 - p))
    put(YIN, between(line, -1, y), turned_by(row_turn[:ny], y))


def mix_columns(left, middle, right, width):
    count = left.shape[0]
    column = lax.broadcasted_iota(jnp.int32, (count, 1), 0) % width
    left = jnp.where(column == 0, 0.0, pltpu.roll(left, 1, 0))
    right = jnp.where(column == width - 1, 0.0, pltpu.roll(right, count - 1, 0))
    return middle + left + right


def taps_of(inputs, weight, taps, width):
    lhs = jnp.concatenate(inputs, axis=1)
    parts = [
        jnp.dot(
            lhs,
            jnp.concatenate([weight[a, b] for a in taps], axis=0),
            preferred_element_type=F32,
        )
        for b in range(3)
    ]
    return mix_columns(*parts, width)


def flat(value):
    return value.reshape(value.shape[0] * value.shape[1], value.shape[2])


def conv_inside(x, w, mod_far, ang_far, acc, tab, mod, ang, sems, *, nx, ny):
    nf, rows, width, _ = x.shape
    copies = [
        pltpu.make_async_copy(mod_far, mod, sems.at[0]),
        pltpu.make_async_copy(ang_far, ang, sems.at[1]),
    ]
    for copy in copies:
        copy.start()
    for r in range(rows):
        if r == rows - 1:
            for copy in copies:
                copy.wait()
            fill_table(mod, ang, tab, nx, ny, nf)
        taps = [a for a in range(3) if 0 <= r + a - 1 < rows]
        acc[r] = taps_of([flat(x[:, r + a - 1]) for a in taps], w, taps, width)


def turned(tab, index, value):
    pairs = value.shape[-1] // 2
    re, im = tab[index, :, :pairs], tab[index, :, pairs:]
    v_re, v_im = value[..., :pairs], value[..., pairs:]
    return jnp.concatenate([re * v_re - im * v_im, im * v_re + re * v_im], axis=-1)


def tiles(value):
    return value.astype(F32).reshape(-1, 8, value.shape[-1])


def finish_update(acc, low, high, w, tab, local, keep, send, top, bottom):
    nf, width, chans = low.shape
    rows = acc.shape[0]
    z, zs = lax.axis_index("row"), lax.axis_size("row")
    c = lax.axis_index(TM[2])
    first = taps_of([flat(low[...])], w, [0], width)
    last = taps_of([flat(high[...])], w, [2], width)
    first = acc[0] + jnp.where(z > 0, first, 0.0)
    last = acc[rows - 1] + jnp.where(z < zs - 1, last, 0.0)
    ends = [None] * rows
    for r in list(range(1, rows - 1)) + [0, rows - 1]:
        update = first if r == 0 else last if r == rows - 1 else acc[r]
        running = None
        for t in range(nf):
            new = tiles(update[t * width : (t + 1) * width])
            running = new if running is None else turned(tab, RATE + t, running) + new
            local[r, t] = running.reshape(width, chans)
            if r == 0:
                top[t] = local[r, t].astype(BF16)
            elif r == rows - 1:
                bottom[t] = local[r, t].astype(BF16)
        ends[r] = running.reshape(width, chans)
    half = rows // 2
    for i in range(half):
        keep[i] = jnp.where(c == 0, ends[i], ends[half + i])
        send[i] = jnp.where(c == 0, ends[half + i], ends[i])


def join_cores(keep, got, tab, chip, start):
    c = lax.axis_index(TM[2])
    for i in range(keep.shape[0]):
        early = jnp.where(c == 0, keep[i], got[i])
        late = jnp.where(c == 0, got[i], keep[i])
        start[i] = early
        total = turned(tab, CORE + 1, tiles(early)) + tiles(late)
        chip[i] = total.reshape(early.shape).astype(BF16)


def join_row(*refs):
    own, *got, tab, prefix, total = refs
    for i in range(own.shape[0]):
        shape = own.shape[1:]
        parts = [tiles(ref[i]) for ref in (own, *got)]
        before = whole = None
        for d, part in enumerate(parts):
            term = turned(tab, XTOT + d, part)
            whole = term if whole is None else whole + term
            if d > 0:
                term = turned(tab, XPRE + d - 1, part)
                before = term if before is None else before + term
        prefix[i] = before.reshape(shape)
        total[i] = whole.reshape(shape).astype(BF16)


def join_all(*refs):
    *got, prefix, start, state_in, tab, keep, send, edge_keep, edge_send = refs
    c = lax.axis_index(TM[2])
    half = prefix.shape[0]
    for i in range(half):
        shape = prefix.shape[1:]
        entry = jnp.where(c == 0, state_in[i], state_in[half + i])
        total = turned(tab, YIN, tiles(entry))
        for d, ref in enumerate(got):
            total = total + turned(tab, YPRE + d, tiles(ref[i]))
        chip = turned(tab, XIN, total) + tiles(prefix[i])
        other = turned(tab, CORE, chip) + tiles(start[i])
        chip, other = chip.reshape(shape), other.reshape(shape)
        keep[i] = jnp.where(c == 0, chip, other)
        send[i] = jnp.where(c == 0, other, chip)
    edge_keep[...] = jnp.where(c == 0, keep[0], keep[half - 1])
    edge_send[...] = jnp.where(c == 0, send[0], send[half - 1])


def states(local, entry, tab):
    nf, width, chans = local.shape
    entry = tiles(entry)
    return jnp.concatenate(
        [
            (tiles(local[t]) + turned(tab, PROD + t, entry)).reshape(width, chans).astype(BF16)
            for t in range(nf)
        ],
        axis=0,
    )


def gelu(v):
    return 0.5 * v * (1.0 + lax.erf(v * (0.5**0.5)))


def conv_state(local, keep, got, tab, w, acc_top, acc_bottom, out):
    rows, nf, width, chans = local.shape
    c = lax.axis_index(TM[2])
    half = rows // 2
    row = []
    for r in range(rows):
        entry = jnp.where(c == r // half, keep[r % half], got[r % half])
        row.append(states(local[r], entry, tab))
    for r in list(range(1, rows - 1)) + [0, rows - 1]:
        taps = [a for a in range(3) if 0 <= r + a - 1 < rows]
        result = taps_of([row[r + a - 1] for a in taps], w, taps, width)
        if r == 0:
            acc_top[...] = result
        elif r == rows - 1:
            acc_bottom[...] = result
        else:
            out[r - 1] = gelu(result).reshape(nf, width, chans).astype(BF16)


def finish_output(
    acc_top, acc_bottom, low, high, same, cross, tab, w, inside, out, edge, sems
):
    nf, width, chans = low.shape
    rows = inside.shape[0] + 2
    z, zs = lax.axis_index("row"), lax.axis_size("row")
    c = lax.axis_index(TM[2])
    copies = []
    for r in range(1, rows - 1):
        copies.append(pltpu.make_async_copy(inside.at[r - 1], out.at[:, r], sems.at[r]))
        copies[-1].start()
    for i, (acc, halo, entry, tap, live, r) in enumerate(
        [
            (acc_top, low, jnp.where(c == 0, cross[...], same[...]), 0, z > 0, 0),
            (acc_bottom, high, jnp.where(c == 0, same[...], cross[...]), 2, z < zs - 1, rows - 1),
        ]
    ):
        part = taps_of([states(halo[...], entry, tab)], w, [tap], width)
        total = acc[...] + jnp.where(live, part, 0.0)
        edge[i] = gelu(total).reshape(nf, width, chans).astype(BF16)
        copies.append(pltpu.make_async_copy(edge.at[i], out.at[:, r], sems.at[r]))
        copies[-1].start()
    for copy in copies:
        copy.wait()


def ring(value, axis, distance):
    count = lax.axis_size(axis)
    return lax.ppermute(value, axis, [(i, (i + distance) % count) for i in range(count)])


def others(value, axis):
    count = lax.axis_size(axis)
    pairs = [[(i, p) for i, p in enumerate(group)] for group in zip(*(
        [int(p) for p in host_partners(i, count)] for i in range(count)
    ))]
    return [lax.ppermute(value, axis, pair) for pair in pairs]


def host_partners(index, count):
    if count == 2:
        return [1 - index]
    return [3 - index, index ^ 1, (index + 2) % 4]


def shards(frames, state_in, modulus, angle, w_in, w_out):
    nf, rows, width, chans = frames.shape
    ny, nx, _ = (lax.axis_size(name) for name in TM)
    zs = lax.axis_size("row")
    half = rows // 2
    far, modulus = (pltpu.with_memory_space_constraint(v, pltpu.HBM) for v in (frames, modulus))
    angle = pltpu.with_memory_space_constraint(angle[None], pltpu.HBM)
    conv_flops = 2 * nf * rows * width * 9 * chans * chans
    conv_bytes = 9 * chans * chans * 2

    def shape(*dims, dtype=F32):
        return jax.ShapeDtypeStruct(dims, dtype)

    row_bf = shape(nf, width, chans, dtype=BF16)
    acc_row = shape(nf * width, chans)
    half_f32 = shape(half, width, chans)
    half_bf = shape(half, width, chans, dtype=BF16)
    one_row = shape(width, chans)

    first, last = call(
        edges,
        (row_bf, row_bf),
        [HBM],
        scratch=[pltpu.SemaphoreType.DMA((2,))],
        flops=conv_flops * 10, size=20 * conv_bytes,
    )(far)
    low = ring(last, "row", 1)
    high = ring(first, "row", -1)
    acc, tab = call(
        functools.partial(conv_inside, nx=nx, ny=ny),
        (shape(rows, nf * width, chans), shape(ROWS, 8, chans)),
        [VM, VM, HBM, HBM],
        scratch=[
            pltpu.VMEM(modulus.shape, F32),
            pltpu.VMEM(angle.shape, F32),
            pltpu.SemaphoreType.DMA((2,)),
        ],
        flops=conv_flops * 10 // 12,
        size=conv_bytes,
    )(frames, w_in, modulus, angle)
    local, keep, send, top, bottom = call(
        finish_update,
        (shape(rows, nf, width, chans), half_f32, half_f32, row_bf, row_bf),
        [VM] * 5,
        flops=conv_flops // 6,
        size=conv_bytes,
    )(acc, low, high, w_in, tab)
    got = ring(send, TM[2], 1)
    low = ring(bottom, "row", 1)
    high = ring(top, "row", -1)
    chip, start = call(join_cores, (half_bf, half_f32), [VM] * 3)(keep, got, tab)
    across = others(chip, TM[1])
    prefix, total = call(join_row, (half_f32, half_bf), [VM] * (nx + 1))(
        chip, *across, tab
    )
    across = others(total, TM[0])
    keep, send, edge_keep, edge_send = call(
        join_all, (half_f32, half_f32, one_row, one_row), [VM] * (ny + 3)
    )(*across, prefix, start, state_in, tab)
    got = ring(send, TM[2], 1)
    step = [-1, 1]
    same, cross = (
        lax.ppermute(
            value,
            (TM[2], "row"),
            [
                (c * zs + z, (c ^ flip) * zs + (z + step[c]) % zs)
                for c in range(2)
                for z in range(zs)
            ],
        )
        for value, flip in ((edge_keep, 0), (edge_send, 1))
    )
    acc_top, acc_bottom, inside = call(
        conv_state,
        (acc_row, acc_row, shape(rows - 2, nf, width, chans, dtype=BF16)),
        [VM] * 5,
        flops=conv_flops * 10 // 12,
        size=conv_bytes,
    )(local, keep, got, tab, w_out)
    return call(
        finish_output,
        shape(nf, rows, width, chans, dtype=BF16),
        [VM] * 9,
        out_specs=HBM,
        scratch=[pltpu.VMEM((2, nf, width, chans), BF16), pltpu.SemaphoreType.DMA((rows,))],
        flops=conv_flops // 6,
        size=conv_bytes,
    )(acc_top, acc_bottom, low, high, same, cross, tab, w_out, inside)


def solution(mesh):
    chips = mesh.shape["tm"] // 2
    side = int(chips**0.5)
    finer = Mesh(
        mesh.devices.reshape(chips // side, side, 2, mesh.shape["row"]), (*TM, "row")
    )
    placed = (P(TM, "row", None, None), P("row", None, None), P(), P(), P(), P())

    return jax.shard_map(
        shards, mesh=finer, in_specs=placed, out_specs=P(TM, "row", None, None), check_vma=False
    )
```

```python
import functools

import jax
import jax.numpy as jnp
from jax import lax
from jax.experimental import pallas as pl
from jax.experimental.pallas import tpu as pltpu
from jax.sharding import Mesh
from jax.sharding import PartitionSpec as P

TM = ("tm_0", "tm_1", "tm_2")
F32 = jnp.float32
BF16 = jnp.bfloat16
VM = pl.BlockSpec(memory_space=pltpu.VMEM)
HBM = pl.BlockSpec(memory_space=pltpu.HBM)

RATE, PROD, CORE, XPRE, XTOT, XIN, YPRE, YIN, ROWS = 0, 4, 8, 10, 13, 17, 18, 21, 22


def call(kernel, outs, specs, out_specs=None, scratch=(), flops=0, size=0, limit=24, aliases=None):
    return pl.pallas_call(
        kernel,
        out_shape=outs,
        in_specs=specs,
        out_specs=out_specs if out_specs is not None else jax.tree.map(lambda _: VM, outs),
        scratch_shapes=list(scratch),
        input_output_aliases=aliases or {},
        cost_estimate=pl.CostEstimate(flops=flops, bytes_accessed=size, transcendentals=0),
        compiler_params=pltpu.CompilerParams(vmem_limit_bytes=limit << 20),
    )


def cmul(a, b):
    return (a[0] * b[0] - a[1] * b[1], a[0] * b[1] + a[1] * b[0])


def partners(index, count):
    if count == 2:
        return [1 - index]
    return [lax.rem(index + 2, 4), index + 1 - 2 * lax.rem(index, 2), 3 - index]


def powers(base, count):
    out = [(jnp.ones_like(base[0]), jnp.zeros_like(base[0]))]
    for _ in range(count):
        out.append(cmul(out[-1], base))
    return out


def edges(frames, first, last, sems):
    rows = frames.shape[1]
    copies = [
        pltpu.make_async_copy(frames.at[:, row], edge, sems.at[i])
        for i, (row, edge) in enumerate([(0, first), (rows - 1, last)])
    ]
    for copy in copies:
        copy.start()
    for copy in copies:
        copy.wait()


def fill_table(mod, ang, tab, nx, ny, nf):
    y, x, c = (lax.axis_index(name) for name in TM)
    pairs = mod.shape[1]
    shape = (8, pairs)
    theta = jnp.broadcast_to(ang[...], shape)
    turn = (jnp.cos(theta), jnp.sin(theta))
    local = powers(turn, nf)
    chip_turn = powers(cmul(local[nf], local[nf]), nx)
    row_turn = powers(chip_turn[nx], ny)

    def put(index, size, angle):
        tab[index, :, :pairs] = size * angle[0]
        tab[index, :, pairs:] = size * angle[1]

    def product8(v):
        v = v * pltpu.roll(v, 7, 0)
        v = v * pltpu.roll(v, 6, 0)
        return v * pltpu.roll(v, 4, 0)

    def chip_rows(index):
        return mod[pl.ds(pl.multiple_of(index * 8, 8), 8), :]

    one = jnp.ones(shape, F32)
    zero = jnp.zeros(shape, F32)
    mine = chip_rows(y * nx + x)
    ms = [jnp.broadcast_to(mine[i : i + 1], shape) for i in range(2 * nf)]
    running = None
    for t in range(nf):
        m = jnp.where(c == 0, ms[t], ms[nf + t])
        running = m if running is None else running * m
        put(RATE + t, m, turn)
        put(PROD + t, running, local[t + 1])
    for core in range(2):
        total = ms[core * nf]
        for t in range(1, nf):
            total = total * ms[core * nf + t]
        put(CORE + core, total, local[nf])
    chips = [product8(chip_rows(y * nx + u)) for u in range(nx)]
    line = []
    for v in range(ny):
        total = product8(chip_rows(v * nx))
        for u in range(1, nx):
            total = total * product8(chip_rows(v * nx + u))
        line.append(total)

    def between(values, low, high):
        total = one
        for u, value in enumerate(values):
            total = total * jnp.where((u > low) & (u < high), value, one)
        return total

    def turned_by(turns, count):
        angle = turns[0]
        for k in range(1, len(turns)):
            angle = tuple(jnp.where(count == k, new, old) for new, old in zip(turns[k], angle))
        return angle

    for i, p in enumerate(partners(x, nx)):
        size = jnp.where(p < x, between(chips, p, x), zero)
        put(XPRE + i, size, turned_by(chip_turn[:nx], x - 1 - p))
    for i, p in enumerate([x, *partners(x, nx)]):
        put(XTOT + i, between(chips, p, nx), turned_by(chip_turn[:nx], nx - 1 - p))
    put(XIN, between(chips, -1, x), turned_by(chip_turn[:nx], x))
    for i, p in enumerate(partners(y, ny)):
        size = jnp.where(p < y, between(line, p, y), zero)
        put(YPRE + i, size, turned_by(row_turn[:ny], y - 1 - p))
    put(YIN, between(line, -1, y), turned_by(row_turn[:ny], y))


def mix_columns(left, middle, right, width):
    count = left.shape[0]
    column = lax.broadcasted_iota(jnp.int32, (count, 1), 0) % width
    left = jnp.where(column == 0, 0.0, pltpu.roll(left, 1, 0))
    right = jnp.where(column == width - 1, 0.0, pltpu.roll(right, count - 1, 0))
    return middle + left + right


def taps_of(inputs, weight, taps, width):
    lhs = jnp.concatenate(inputs, axis=1)
    parts = [
        jnp.dot(
            lhs,
            jnp.concatenate([weight[a, b] for a in taps], axis=0),
            preferred_element_type=F32,
        )
        for b in range(3)
    ]
    return mix_columns(*parts, width)


def flat(value):
    return value.reshape(value.shape[0] * value.shape[1], value.shape[2])


def turned(tab, index, value):
    pairs = value.shape[-1] // 2
    re, im = tab[index, :, :pairs], tab[index, :, pairs:]
    v_re, v_im = value[..., :pairs], value[..., pairs:]
    return jnp.concatenate([re * v_re - im * v_im, im * v_re + re * v_im], axis=-1)


def tiles(value):
    return value.astype(F32).reshape(-1, 8, value.shape[-1])


def scan(update, tab, local, row, width):
    nf, chans = local.shape[1], local.shape[3]
    running = None
    for t in range(nf):
        new = tiles(update[t * width : (t + 1) * width])
        running = new if running is None else turned(tab, RATE + t, running) + new
        local[row, t] = running.reshape(width, chans)
    return running.reshape(width, chans)


def share(ends, keep, send):
    c = lax.axis_index(TM[2])
    keep[...] = jnp.where(c == 0, ends[0], ends[1])
    send[...] = jnp.where(c == 0, ends[1], ends[0])


def update_inner(x, w, mod_far, ang_far, local, keep, send, tab, mod, ang, sems, *, nx, ny):
    nf, rows, width, _ = x.shape
    copies = [
        pltpu.make_async_copy(mod_far, mod, sems.at[0]),
        pltpu.make_async_copy(ang_far, ang, sems.at[1]),
    ]
    for copy in copies:
        copy.start()
    updates = [
        taps_of([flat(x[:, r + a - 1]) for a in range(3)], w, range(3), width)
        for r in range(1, rows - 1)
    ]
    for copy in copies:
        copy.wait()
    fill_table(mod, ang, tab, nx, ny, nf)
    share([scan(update, tab, local, i, width) for i, update in enumerate(updates)], keep, send)


def update_outer(x, w, acc):
    _, rows, width, _ = x.shape
    acc[0] = taps_of([flat(x[:, 0]), flat(x[:, 1])], w, [1, 2], width)
    acc[1] = taps_of([flat(x[:, rows - 2]), flat(x[:, rows - 1])], w, [0, 1], width)


def finish_outer(acc, low, high, w, tab, local, keep, send, top, bottom):
    width = low.shape[1]
    z, zs = lax.axis_index("row"), lax.axis_size("row")
    first = taps_of([flat(low[...])], w, [0], width)
    last = taps_of([flat(high[...])], w, [2], width)
    ends = [
        scan(acc[0] + jnp.where(z > 0, first, 0.0), tab, local, 0, width),
        scan(acc[1] + jnp.where(z < zs - 1, last, 0.0), tab, local, 1, width),
    ]
    share(ends, keep, send)
    top[...] = local[0].astype(BF16)
    bottom[...] = local[1].astype(BF16)


def join_cores(keep, got, tab, chip, start):
    c = lax.axis_index(TM[2])
    early = jnp.where(c == 0, keep[...], got[...])
    late = jnp.where(c == 0, got[...], keep[...])
    start[...] = early
    total = turned(tab, CORE + 1, tiles(early)) + tiles(late)
    chip[...] = total.reshape(early.shape).astype(BF16)


def join_row(*refs):
    own, *got, tab, prefix, total = refs
    before = whole = None
    for d, ref in enumerate((own, *got)):
        part = tiles(ref[...])
        term = turned(tab, XTOT + d, part)
        whole = term if whole is None else whole + term
        if d > 0:
            term = turned(tab, XPRE + d - 1, part)
            before = term if before is None else before + term
    prefix[...] = before.reshape(own.shape)
    total[...] = whole.reshape(own.shape).astype(BF16)


def join_all(*refs, rows):
    *got, prefix, start, state_in, tab, keep, send = refs
    c = lax.axis_index(TM[2])
    entry = jnp.where(c == 0, state_in[rows[0]], state_in[rows[1]])
    total = turned(tab, YIN, tiles(entry))
    for d, ref in enumerate(got):
        total = total + turned(tab, YPRE + d, tiles(ref[...]))
    chip = turned(tab, XIN, total) + tiles(prefix[...])
    other = turned(tab, CORE, chip) + tiles(start[...])
    chip, other = chip.reshape(prefix.shape), other.reshape(prefix.shape)
    keep[...] = jnp.where(c == 0, chip, other)
    send[...] = jnp.where(c == 0, other, chip)


def states(local, entry, tab):
    nf, width, chans = local.shape
    entry = tiles(entry)
    return jnp.concatenate(
        [
            (tiles(local[t]) + turned(tab, PROD + t, entry)).reshape(width, chans).astype(BF16)
            for t in range(nf)
        ],
        axis=0,
    )


def gelu(v):
    return 0.5 * v * (1.0 + lax.erf(v * (0.5**0.5)))


def conv_state(
    inner, outer, keep_in, got_in, keep_out, got_out, tab, w, acc_top, acc_bottom, out
):
    _, nf, width, chans = inner.shape
    rows = 4
    c = lax.axis_index(TM[2])
    row = []
    for local, i, keep, got in (
        (outer, 0, keep_out, got_out),
        (inner, 0, keep_in, got_in),
        (inner, 1, keep_in, got_in),
        (outer, 1, keep_out, got_out),
    ):
        row.append(states(local[i], jnp.where(c == i, keep[...], got[...]), tab))
    for r in list(range(1, rows - 1)) + [0, rows - 1]:
        taps = [a for a in range(3) if 0 <= r + a - 1 < rows]
        result = taps_of([row[r + a - 1] for a in taps], w, taps, width)
        if r == 0:
            acc_top[...] = result
        elif r == rows - 1:
            acc_bottom[...] = result
        else:
            out[r - 1] = gelu(result).reshape(nf, width, chans).astype(BF16)


def finish_output(
    acc_top, acc_bottom, low, high, same, cross, tab, w, inside, out, edge, sems
):
    nf, width, chans = low.shape
    rows = inside.shape[0] + 2
    z, zs = lax.axis_index("row"), lax.axis_size("row")
    c = lax.axis_index(TM[2])
    copies = []
    for r in range(1, rows - 1):
        copies.append(pltpu.make_async_copy(inside.at[r - 1], out.at[:, r], sems.at[r]))
        copies[-1].start()
    for i, (acc, halo, entry, tap, live, r) in enumerate(
        [
            (acc_top, low, jnp.where(c == 0, cross[...], same[...]), 0, z > 0, 0),
            (acc_bottom, high, jnp.where(c == 0, same[...], cross[...]), 2, z < zs - 1, rows - 1),
        ]
    ):
        part = taps_of([states(halo[...], entry, tab)], w, [tap], width)
        total = acc[...] + jnp.where(live, part, 0.0)
        edge[i] = gelu(total).reshape(nf, width, chans).astype(BF16)
        copies.append(pltpu.make_async_copy(edge.at[i], out.at[:, r], sems.at[r]))
        copies[-1].start()
    for copy in copies:
        copy.wait()


def ring(value, axis, distance):
    count = lax.axis_size(axis)
    return lax.ppermute(value, axis, [(i, (i + distance) % count) for i in range(count)])


def others(value, axis):
    count = lax.axis_size(axis)
    pairs = [[(i, p) for i, p in enumerate(group)] for group in zip(*(
        [int(p) for p in host_partners(i, count)] for i in range(count)
    ))]
    return [lax.ppermute(value, axis, pair) for pair in pairs]


def host_partners(index, count):
    if count == 2:
        return [1 - index]
    return [(index + 2) % 4, index ^ 1, 3 - index]


def shards(frames, state_in, modulus, angle, w_in, w_out):
    nf, rows, width, chans = frames.shape
    ny, nx, _ = (lax.axis_size(name) for name in TM)
    zs = lax.axis_size("row")
    far, modulus = (pltpu.with_memory_space_constraint(v, pltpu.HBM) for v in (frames, modulus))
    angle = pltpu.with_memory_space_constraint(angle[None], pltpu.HBM)
    conv_flops = 2 * nf * rows * width * 9 * chans * chans
    conv_bytes = 9 * chans * chans * 2

    def shape(*dims, dtype=F32):
        return jax.ShapeDtypeStruct(dims, dtype)

    row_bf = shape(nf, width, chans, dtype=BF16)
    acc_row = shape(nf * width, chans)
    one_row = shape(width, chans)
    one_bf = shape(width, chans, dtype=BF16)
    two_rows = shape(2, nf, width, chans)

    first, last = call(
        edges,
        (row_bf, row_bf),
        [HBM],
        scratch=[pltpu.SemaphoreType.DMA((2,))],
        flops=conv_flops * 10,
        size=20 * conv_bytes,
    )(far)
    low = ring(last, "row", 1)
    high = ring(first, "row", -1)

    def gather(chip, start, rows):
        across = others(chip, TM[1])
        prefix, total = call(join_row, (one_row, one_bf), [VM] * (nx + 1))(chip, *across, tab)
        across = others(total, TM[0])
        keep, send = call(
            functools.partial(join_all, rows=rows), (one_row, one_row), [VM] * (ny + 3)
        )(*across, prefix, start, state_in, tab)
        return keep, send, ring(send, TM[2], 1)

    inner, keep, send, tab = call(
        functools.partial(update_inner, nx=nx, ny=ny),
        (two_rows, one_row, one_row, shape(ROWS, 8, chans)),
        [VM, VM, HBM, HBM],
        scratch=[
            pltpu.VMEM(modulus.shape, F32),
            pltpu.VMEM(angle.shape, F32),
            pltpu.SemaphoreType.DMA((2,)),
        ],
        flops=conv_flops // 2,
        size=conv_bytes,
    )(frames, w_in, modulus, angle)
    got = ring(send, TM[2], 1)
    acc = call(
        update_outer,
        shape(2, nf * width, chans),
        [VM, VM],
        flops=conv_flops // 3,
        size=conv_bytes,
    )(frames, w_in)
    chip, start = call(join_cores, (one_bf, one_row), [VM] * 3)(keep, got, tab)
    keep_in, _, got_in = gather(chip, start, (1, 2))

    outer, keep, send, top, bottom = call(
        finish_outer,
        (two_rows, one_row, one_row, row_bf, row_bf),
        [VM] * 5,
        flops=conv_flops // 6,
        size=conv_bytes,
    )(acc, low, high, w_in, tab)
    got = ring(send, TM[2], 1)
    low = ring(bottom, "row", 1)
    high = ring(top, "row", -1)
    chip, start = call(join_cores, (one_bf, one_row), [VM] * 3)(keep, got, tab)
    keep_out, send, got_out = gather(chip, start, (0, 3))
    step = [-1, 1]
    same, cross = (
        lax.ppermute(
            value,
            (TM[2], "row"),
            [
                (c * zs + z, (c ^ flip) * zs + (z + step[c]) % zs)
                for c in range(2)
                for z in range(zs)
            ],
        )
        for value, flip in ((keep_out, 0), (send, 1))
    )
    acc_top, acc_bottom, inside = call(
        conv_state,
        (acc_row, acc_row, shape(rows - 2, nf, width, chans, dtype=BF16)),
        [VM] * 8,
        flops=conv_flops * 10 // 12,
        size=conv_bytes,
    )(inner, outer, keep_in, got_in, keep_out, got_out, tab, w_out)
    return call(
        finish_output,
        shape(nf, rows, width, chans, dtype=BF16),
        [VM] * 9,
        out_specs=HBM,
        scratch=[pltpu.VMEM((2, nf, width, chans), BF16), pltpu.SemaphoreType.DMA((rows,))],
        flops=conv_flops // 6,
        size=conv_bytes,
    )(acc_top, acc_bottom, low, high, same, cross, tab, w_out, inside)


def solution(mesh):
    chips = mesh.shape["tm"] // 2
    side = int(chips**0.5)
    finer = Mesh(
        mesh.devices.reshape(chips // side, side, 2, mesh.shape["row"]), (*TM, "row")
    )
    placed = (P(TM, "row", None, None), P("row", None, None), P(), P(), P(), P())

    return jax.shard_map(
        shards, mesh=finer, in_specs=placed, out_specs=P(TM, "row", None, None), check_vma=False
    )
```

```python
import functools

import jax
import jax.numpy as jnp
from jax import lax
from jax.experimental import pallas as pl
from jax.experimental.pallas import tpu as pltpu
from jax.sharding import Mesh
from jax.sharding import PartitionSpec as P

TM = ("tm_0", "tm_1", "tm_2")
F32 = jnp.float32
BF16 = jnp.bfloat16
VM = pl.BlockSpec(memory_space=pltpu.VMEM)
HBM = pl.BlockSpec(memory_space=pltpu.HBM)

RATE, PROD, CORE, XPRE, XTOT, XIN, YPRE, YIN, XPAIR, YPAIR, ROWS = 0, 4, 8, 10, 13, 17, 18, 21, 22, 28, 34


def call(kernel, outs, specs, out_specs=None, scratch=(), flops=0, size=0, limit=24, aliases=None):
    return pl.pallas_call(
        kernel,
        out_shape=outs,
        in_specs=specs,
        out_specs=out_specs if out_specs is not None else jax.tree.map(lambda _: VM, outs),
        scratch_shapes=list(scratch),
        input_output_aliases=aliases or {},
        cost_estimate=pl.CostEstimate(flops=flops, bytes_accessed=size, transcendentals=0),
        compiler_params=pltpu.CompilerParams(vmem_limit_bytes=limit << 20),
    )


def cmul(a, b):
    return (a[0] * b[0] - a[1] * b[1], a[0] * b[1] + a[1] * b[0])


def partners(index, count):
    if count == 2:
        return [1 - index]
    return [lax.rem(index + 2, 4), index + 1 - 2 * lax.rem(index, 2), 3 - index]


def powers(base, count):
    out = [(jnp.ones_like(base[0]), jnp.zeros_like(base[0]))]
    for _ in range(count):
        out.append(cmul(out[-1], base))
    return out


def edges(frames, first, last, sems):
    rows = frames.shape[1]
    copies = [
        pltpu.make_async_copy(frames.at[:, row], edge, sems.at[i])
        for i, (row, edge) in enumerate([(0, first), (rows - 1, last)])
    ]
    for copy in copies:
        copy.start()
    for copy in copies:
        copy.wait()


def fill_table(mod, ang, tab, nx, ny, nf):
    y, x, c = (lax.axis_index(name) for name in TM)
    pairs = mod.shape[1]
    shape = (8, pairs)
    theta = jnp.broadcast_to(ang[...], shape)
    turn = (jnp.cos(theta), jnp.sin(theta))
    local = powers(turn, nf)
    chip_turn = powers(cmul(local[nf], local[nf]), nx)
    row_turn = powers(chip_turn[nx], ny)

    def put(index, size, angle):
        tab[index, :, :pairs] = size * angle[0]
        tab[index, :, pairs:] = size * angle[1]

    def product8(v):
        v = v * pltpu.roll(v, 7, 0)
        v = v * pltpu.roll(v, 6, 0)
        return v * pltpu.roll(v, 4, 0)

    def chip_rows(index):
        return mod[pl.ds(pl.multiple_of(index * 8, 8), 8), :]

    one = jnp.ones(shape, F32)
    zero = jnp.zeros(shape, F32)
    mine = chip_rows(y * nx + x)
    ms = [jnp.broadcast_to(mine[i : i + 1], shape) for i in range(2 * nf)]
    running = None
    for t in range(nf):
        m = jnp.where(c == 0, ms[t], ms[nf + t])
        running = m if running is None else running * m
        put(RATE + t, m, turn)
        put(PROD + t, running, local[t + 1])
    for core in range(2):
        total = ms[core * nf]
        for t in range(1, nf):
            total = total * ms[core * nf + t]
        put(CORE + core, total, local[nf])
    chips = [product8(chip_rows(y * nx + u)) for u in range(nx)]
    line = []
    for v in range(ny):
        total = product8(chip_rows(v * nx))
        for u in range(1, nx):
            total = total * product8(chip_rows(v * nx + u))
        line.append(total)

    def between(values, low, high):
        total = one
        for u, value in enumerate(values):
            total = total * jnp.where((u > low) & (u < high), value, one)
        return total

    def turned_by(turns, count):
        angle = turns[0]
        for k in range(1, len(turns)):
            angle = tuple(jnp.where(count == k, new, old) for new, old in zip(turns[k], angle))
        return angle

    for i, p in enumerate(partners(x, nx)):
        size = jnp.where(p < x, between(chips, p, x), zero)
        put(XPRE + i, size, turned_by(chip_turn[:nx], x - 1 - p))
    for i, p in enumerate([x, *partners(x, nx)]):
        put(XTOT + i, between(chips, p, nx), turned_by(chip_turn[:nx], nx - 1 - p))
    put(XIN, between(chips, -1, x), turned_by(chip_turn[:nx], x))
    for i, p in enumerate(partners(y, ny)):
        size = jnp.where(p < y, between(line, p, y), zero)
        put(YPRE + i, size, turned_by(row_turn[:ny], y - 1 - p))
    put(YIN, between(line, -1, y), turned_by(row_turn[:ny], y))

    def select(flag, new, old):
        return tuple(jnp.where(flag, a, b) for a, b in zip(new, old))

    def pairwise(index, values, turns, place):
        unit, nothing = (one, zero), (zero, zero)
        late = lax.rem(index, 2) == 1
        rates = [(value * turns[1][0], value * turns[1][1]) for value in values]
        upper = rates[1]
        if len(values) == 4:
            upper = select(index >= 2, rates[3], rates[1])
        steps = [(select(late, upper, unit), select(late, unit, upper), select(late, unit, nothing))]
        if len(values) == 4:
            late = index >= 2
            block = values[2] * values[3]
            block = (block * turns[2][0], block * turns[2][1])
            before = select(index == 3, rates[2], select(index == 2, unit, nothing))
            steps.append((select(late, block, unit), select(late, unit, block), before))
        for i, factor in enumerate(f for step in steps for f in step):
            put(place + i, one, factor)

    pairwise(x, chips, chip_turn, XPAIR)
    pairwise(y, line, row_turn, YPAIR)


def mix_columns(left, middle, right, width):
    count = left.shape[0]
    column = lax.broadcasted_iota(jnp.int32, (count, 1), 0) % width
    left = jnp.where(column == 0, 0.0, pltpu.roll(left, 1, 0))
    right = jnp.where(column == width - 1, 0.0, pltpu.roll(right, count - 1, 0))
    return middle + left + right


def taps_of(inputs, weight, taps, width):
    lhs = jnp.concatenate(inputs, axis=1)
    parts = [
        jnp.dot(
            lhs,
            jnp.concatenate([weight[a, b] for a in taps], axis=0),
            preferred_element_type=F32,
        )
        for b in range(3)
    ]
    return mix_columns(*parts, width)


def flat(value):
    return value.reshape(value.shape[0] * value.shape[1], value.shape[2])


def turned(tab, index, value):
    pairs = value.shape[-1] // 2
    re, im = tab[index, :, :pairs], tab[index, :, pairs:]
    v_re, v_im = value[..., :pairs], value[..., pairs:]
    return jnp.concatenate([re * v_re - im * v_im, im * v_re + re * v_im], axis=-1)


def tiles(value):
    return value.astype(F32).reshape(-1, 8, value.shape[-1])


def scan(update, tab, local, row, width):
    nf, chans = local.shape[1], local.shape[3]
    running = None
    for t in range(nf):
        new = tiles(update[t * width : (t + 1) * width])
        running = new if running is None else turned(tab, RATE + t, running) + new
        local[row, t] = running.reshape(width, chans)
    return running.reshape(width, chans)


def share(ends, keep, send):
    c = lax.axis_index(TM[2])
    keep[...] = jnp.where(c == 0, ends[0], ends[1])
    send[...] = jnp.where(c == 0, ends[1], ends[0])


def update_inner(x, w, mod_far, ang_far, local, keep, send, tab, mod, ang, sems, *, nx, ny):
    nf, rows, width, _ = x.shape
    copies = [
        pltpu.make_async_copy(mod_far, mod, sems.at[0]),
        pltpu.make_async_copy(ang_far, ang, sems.at[1]),
    ]
    for copy in copies:
        copy.start()
    updates = [
        taps_of([flat(x[:, r + a - 1]) for a in range(3)], w, range(3), width)
        for r in range(1, rows - 1)
    ]
    for copy in copies:
        copy.wait()
    fill_table(mod, ang, tab, nx, ny, nf)
    share([scan(update, tab, local, i, width) for i, update in enumerate(updates)], keep, send)


def update_outer(x, w, acc):
    _, rows, width, _ = x.shape
    acc[0] = taps_of([flat(x[:, 0]), flat(x[:, 1])], w, [1, 2], width)
    acc[1] = taps_of([flat(x[:, rows - 2]), flat(x[:, rows - 1])], w, [0, 1], width)


def finish_outer(acc, low, high, w, tab, local, keep, send, top, bottom):
    width = low.shape[1]
    z, zs = lax.axis_index("row"), lax.axis_size("row")
    first = taps_of([flat(low[...])], w, [0], width)
    last = taps_of([flat(high[...])], w, [2], width)
    ends = [
        scan(acc[0] + jnp.where(z > 0, first, 0.0), tab, local, 0, width),
        scan(acc[1] + jnp.where(z < zs - 1, last, 0.0), tab, local, 1, width),
    ]
    share(ends, keep, send)
    top[...] = local[0].astype(BF16)
    bottom[...] = local[1].astype(BF16)


def join_cores(keep, got, tab, start, *chip):
    c = lax.axis_index(TM[2])
    early = jnp.where(c == 0, keep[...], got[...])
    late = jnp.where(c == 0, got[...], keep[...])
    start[...] = early
    total = turned(tab, CORE + 1, tiles(early)) + tiles(late)
    for ref in chip:
        ref[...] = total.reshape(early.shape).astype(ref.dtype)


def join_pair(own, got, *refs, place, first):
    tab, prefix, total, message = refs[-4:]
    part = tiles(got[...])
    whole = turned(tab, place, part) + turned(tab, place + 1, tiles(own[...]))
    before = turned(tab, place + 2, part)
    if not first:
        before = before + tiles(refs[0][...])
    prefix[...] = before.reshape(prefix.shape)
    total[...] = whole.reshape(total.shape)
    message[...] = whole.reshape(total.shape).astype(BF16)


def join_row(*refs):
    own, *got, tab, prefix, total = refs
    before = whole = None
    for d, ref in enumerate((own, *got)):
        part = tiles(ref[...])
        term = turned(tab, XTOT + d, part)
        whole = term if whole is None else whole + term
        if d > 0:
            term = turned(tab, XPRE + d - 1, part)
            before = term if before is None else before + term
    prefix[...] = before.reshape(own.shape)
    total[...] = whole.reshape(own.shape).astype(BF16)


def entry_of(before, prefix, start, state_in, tab, rows):
    c = lax.axis_index(TM[2])
    entry = jnp.where(c == 0, state_in[rows[0]], state_in[rows[1]])
    total = turned(tab, YIN, tiles(entry)) + before
    chip = turned(tab, XIN, total) + tiles(prefix[...])
    other = turned(tab, CORE, chip) + tiles(start[...])
    chip, other = chip.reshape(prefix.shape), other.reshape(prefix.shape)
    return jnp.where(c == 0, chip, other), jnp.where(c == 0, other, chip)


def join_inner(got, *refs, place):
    *earlier, prefix, start, state_in, tab, keep, send = refs
    before = turned(tab, place + 2, tiles(got[...]))
    for ref in earlier:
        before = before + tiles(ref[...])
    keep[...], send[...] = entry_of(before, prefix, start, state_in, tab, (1, 2))


def join_outer(*refs):
    *got, prefix, start, state_in, tab, send_in, keep, send, both = refs
    before = None
    for d, ref in enumerate(got):
        term = turned(tab, YPRE + d, tiles(ref[...]))
        before = term if before is None else before + term
    keep[...], send[...] = entry_of(before, prefix, start, state_in, tab, (0, 3))
    both[0] = send_in[...]
    both[1] = send[...]


def states(local, entry, tab):
    nf, width, chans = local.shape
    entry = tiles(entry)
    return jnp.concatenate(
        [
            (tiles(local[t]) + turned(tab, PROD + t, entry)).reshape(width, chans).astype(BF16)
            for t in range(nf)
        ],
        axis=0,
    )


def gelu(v):
    return 0.5 * v * (1.0 + lax.erf(v * (0.5**0.5)))


def conv_state(
    inner, outer, keep_in, keep_out, got, tab, w, acc_top, acc_bottom, out
):
    _, nf, width, chans = inner.shape
    rows = 4
    c = lax.axis_index(TM[2])
    row = []
    for local, i, keep, group in (
        (outer, 0, keep_out, 1),
        (inner, 0, keep_in, 0),
        (inner, 1, keep_in, 0),
        (outer, 1, keep_out, 1),
    ):
        row.append(states(local[i], jnp.where(c == i, keep[...], got[group]), tab))
    for r in list(range(1, rows - 1)) + [0, rows - 1]:
        taps = [a for a in range(3) if 0 <= r + a - 1 < rows]
        result = taps_of([row[r + a - 1] for a in taps], w, taps, width)
        if r == 0:
            acc_top[...] = result
        elif r == rows - 1:
            acc_bottom[...] = result
        else:
            out[r - 1] = gelu(result).reshape(nf, width, chans).astype(BF16)


def finish_output(
    acc_top, acc_bottom, low, high, same, cross, tab, w, inside, out, edge, sems
):
    nf, width, chans = low.shape
    rows = inside.shape[0] + 2
    z, zs = lax.axis_index("row"), lax.axis_size("row")
    c = lax.axis_index(TM[2])
    copies = []
    for r in range(1, rows - 1):
        copies.append(pltpu.make_async_copy(inside.at[r - 1], out.at[:, r], sems.at[r]))
        copies[-1].start()
    for i, (acc, halo, entry, tap, live, r) in enumerate(
        [
            (acc_top, low, jnp.where(c == 0, cross[...], same[...]), 0, z > 0, 0),
            (acc_bottom, high, jnp.where(c == 0, same[...], cross[...]), 2, z < zs - 1, rows - 1),
        ]
    ):
        part = taps_of([states(halo[...], entry, tab)], w, [tap], width)
        total = acc[...] + jnp.where(live, part, 0.0)
        edge[i] = gelu(total).reshape(nf, width, chans).astype(BF16)
        copies.append(pltpu.make_async_copy(edge.at[i], out.at[:, r], sems.at[r]))
        copies[-1].start()
    for copy in copies:
        copy.wait()


def ring(value, axis, distance):
    count = lax.axis_size(axis)
    return lax.ppermute(value, axis, [(i, (i + distance) % count) for i in range(count)])


def others(value, axis):
    count = lax.axis_size(axis)
    pairs = [[(i, p) for i, p in enumerate(group)] for group in zip(*(
        [int(p) for p in host_partners(i, count)] for i in range(count)
    ))]
    return [lax.ppermute(value, axis, pair) for pair in pairs]


def host_partners(index, count):
    if count == 2:
        return [1 - index]
    return [(index + 2) % 4, index ^ 1, 3 - index]


def shards(frames, state_in, modulus, angle, w_in, w_out):
    nf, rows, width, chans = frames.shape
    ny, nx, _ = (lax.axis_size(name) for name in TM)
    zs = lax.axis_size("row")
    far, modulus = (pltpu.with_memory_space_constraint(v, pltpu.HBM) for v in (frames, modulus))
    angle = pltpu.with_memory_space_constraint(angle[None], pltpu.HBM)
    conv_flops = 2 * nf * rows * width * 9 * chans * chans
    conv_bytes = 9 * chans * chans * 2

    def shape(*dims, dtype=F32):
        return jax.ShapeDtypeStruct(dims, dtype)

    row_bf = shape(nf, width, chans, dtype=BF16)
    acc_row = shape(nf * width, chans)
    one_row = shape(width, chans)
    one_bf = shape(width, chans, dtype=BF16)
    two_rows = shape(2, nf, width, chans)

    first, last = call(
        edges,
        (row_bf, row_bf),
        [HBM],
        scratch=[pltpu.SemaphoreType.DMA((2,))],
        flops=conv_flops * 10,
        size=20 * conv_bytes,
    )(far)
    low = ring(last, "row", 1)
    high = ring(first, "row", -1)

    def pair_steps(own, message, axis, place, keep_last):
        count = lax.axis_size(axis)
        partner = [lambda i: i ^ 1, lambda i: 3 - i][: 1 if count == 2 else 2]
        prefix = []
        for i, of in enumerate(partner):
            got = lax.ppermute(message, axis, [(k, of(k)) for k in range(count)])
            if keep_last and i == len(partner) - 1:
                return got, prefix, place + 3 * i
            before, own, message = call(
                functools.partial(join_pair, place=place + 3 * i, first=i == 0),
                (one_row, one_row, one_bf),
                [VM] * (3 + len(prefix)),
            )(own, got, *prefix, tab)
            prefix = [before]
        return own, message, before

    inner, keep, send, tab = call(
        functools.partial(update_inner, nx=nx, ny=ny),
        (two_rows, one_row, one_row, shape(ROWS, 8, chans)),
        [VM, VM, HBM, HBM],
        scratch=[
            pltpu.VMEM(modulus.shape, F32),
            pltpu.VMEM(angle.shape, F32),
            pltpu.SemaphoreType.DMA((2,)),
        ],
        flops=conv_flops // 2,
        size=conv_bytes,
    )(frames, w_in, modulus, angle)
    got = ring(send, TM[2], 1)
    acc = call(
        update_outer,
        shape(2, nf * width, chans),
        [VM, VM],
        flops=conv_flops // 3,
        size=conv_bytes,
    )(frames, w_in)
    start, own, message = call(join_cores, (one_row, one_row, one_bf), [VM] * 3)(keep, got, tab)
    own, message, prefix = pair_steps(own, message, TM[1], XPAIR, False)
    got, before, place = pair_steps(own, message, TM[0], YPAIR, True)
    keep_in, send_in = call(
        functools.partial(join_inner, place=place), (one_row, one_row), [VM] * (5 + len(before))
    )(got, *before, prefix, start, state_in, tab)

    outer, keep, send, top, bottom = call(
        finish_outer,
        (two_rows, one_row, one_row, row_bf, row_bf),
        [VM] * 5,
        flops=conv_flops // 6,
        size=conv_bytes,
    )(acc, low, high, w_in, tab)
    got = ring(send, TM[2], 1)
    low = ring(bottom, "row", 1)
    high = ring(top, "row", -1)
    start, chip = call(join_cores, (one_row, one_bf), [VM] * 3)(keep, got, tab)
    across = others(chip, TM[1])
    prefix, total = call(join_row, (one_row, one_bf), [VM] * (nx + 1))(chip, *across, tab)
    across = others(total, TM[0])
    keep_out, send, both = call(
        join_outer, (one_row, one_row, shape(2, width, chans)), [VM] * (ny + 4)
    )(*across, prefix, start, state_in, tab, send_in)
    got = ring(both, TM[2], 1)
    step = [-1, 1]
    same, cross = (
        lax.ppermute(
            value,
            (TM[2], "row"),
            [
                (c * zs + z, (c ^ flip) * zs + (z + step[c]) % zs)
                for c in range(2)
                for z in range(zs)
            ],
        )
        for value, flip in ((keep_out, 0), (send, 1))
    )
    acc_top, acc_bottom, inside = call(
        conv_state,
        (acc_row, acc_row, shape(rows - 2, nf, width, chans, dtype=BF16)),
        [VM] * 7,
        flops=conv_flops * 10 // 12,
        size=conv_bytes,
    )(inner, outer, keep_in, keep_out, got, tab, w_out)
    return call(
        finish_output,
        shape(nf, rows, width, chans, dtype=BF16),
        [VM] * 9,
        out_specs=HBM,
        scratch=[pltpu.VMEM((2, nf, width, chans), BF16), pltpu.SemaphoreType.DMA((rows,))],
        flops=conv_flops // 6,
        size=conv_bytes,
    )(acc_top, acc_bottom, low, high, same, cross, tab, w_out, inside)


def solution(mesh):
    chips = mesh.shape["tm"] // 2
    side = int(chips**0.5)
    finer = Mesh(
        mesh.devices.reshape(chips // side, side, 2, mesh.shape["row"]), (*TM, "row")
    )
    placed = (P(TM, "row", None, None), P("row", None, None), P(), P(), P(), P())

    return jax.shard_map(
        shards, mesh=finer, in_specs=placed, out_specs=P(TM, "row", None, None), check_vma=False
    )
```

```python
import functools

import jax
import jax.numpy as jnp
from jax import lax
from jax.experimental import pallas as pl
from jax.experimental.pallas import tpu as pltpu
from jax.sharding import Mesh
from jax.sharding import PartitionSpec as P

TM = ("tm_0", "tm_1", "tm_2")
F32 = jnp.float32
BF16 = jnp.bfloat16
VM = pl.BlockSpec(memory_space=pltpu.VMEM)
HBM = pl.BlockSpec(memory_space=pltpu.HBM)

RATE, PROD, CORE, XPRE, XTOT, XIN, YPRE, YIN, XPAIR, YPAIR, ROWS = 0, 4, 8, 10, 13, 17, 18, 21, 22, 28, 34


def call(kernel, outs, specs, out_specs=None, scratch=(), flops=0, size=0, limit=24, aliases=None):
    return pl.pallas_call(
        kernel,
        out_shape=outs,
        in_specs=specs,
        out_specs=out_specs if out_specs is not None else jax.tree.map(lambda _: VM, outs),
        scratch_shapes=list(scratch),
        input_output_aliases=aliases or {},
        cost_estimate=pl.CostEstimate(flops=flops, bytes_accessed=size, transcendentals=0),
        compiler_params=pltpu.CompilerParams(vmem_limit_bytes=limit << 20),
    )


def cmul(a, b):
    return (a[0] * b[0] - a[1] * b[1], a[0] * b[1] + a[1] * b[0])


def partners(index, count):
    if count == 2:
        return [1 - index]
    return [lax.rem(index + 2, 4), index + 1 - 2 * lax.rem(index, 2), 3 - index]


def powers(base, count):
    out = [(jnp.ones_like(base[0]), jnp.zeros_like(base[0]))]
    for _ in range(count):
        out.append(cmul(out[-1], base))
    return out


def edges(frames, first, last, sems):
    rows = frames.shape[1]
    copies = [
        pltpu.make_async_copy(frames.at[:, row], edge, sems.at[i])
        for i, (row, edge) in enumerate([(0, first), (rows - 1, last)])
    ]
    for copy in copies:
        copy.start()
    for copy in copies:
        copy.wait()


def fill_table(mod, ang, tab, nx, ny, nf):
    y, x, c = (lax.axis_index(name) for name in TM)
    pairs = mod.shape[1]
    shape = (8, pairs)
    theta = jnp.broadcast_to(ang[...], shape)
    turn = (jnp.cos(theta), jnp.sin(theta))
    local = powers(turn, nf)
    chip_turn = powers(cmul(local[nf], local[nf]), nx)
    row_turn = powers(chip_turn[nx], ny)

    def put(index, size, angle):
        tab[index, :, :pairs] = size * angle[0]
        tab[index, :, pairs:] = size * angle[1]

    def product8(v):
        v = v * pltpu.roll(v, 7, 0)
        v = v * pltpu.roll(v, 6, 0)
        return v * pltpu.roll(v, 4, 0)

    def chip_rows(index):
        return mod[pl.ds(pl.multiple_of(index * 8, 8), 8), :]

    one = jnp.ones(shape, F32)
    zero = jnp.zeros(shape, F32)
    mine = chip_rows(y * nx + x)
    ms = [jnp.broadcast_to(mine[i : i + 1], shape) for i in range(2 * nf)]
    running = None
    for t in range(nf):
        m = jnp.where(c == 0, ms[t], ms[nf + t])
        running = m if running is None else running * m
        put(RATE + t, m, turn)
        put(PROD + t, running, local[t + 1])
    for core in range(2):
        total = ms[core * nf]
        for t in range(1, nf):
            total = total * ms[core * nf + t]
        put(CORE + core, total, local[nf])
    chips = [product8(chip_rows(y * nx + u)) for u in range(nx)]
    line = []
    for v in range(ny):
        total = product8(chip_rows(v * nx))
        for u in range(1, nx):
            total = total * product8(chip_rows(v * nx + u))
        line.append(total)

    def between(values, low, high):
        total = one
        for u, value in enumerate(values):
            total = total * jnp.where((u > low) & (u < high), value, one)
        return total

    def turned_by(turns, count):
        angle = turns[0]
        for k in range(1, len(turns)):
            angle = tuple(jnp.where(count == k, new, old) for new, old in zip(turns[k], angle))
        return angle

    for i, p in enumerate(partners(x, nx)):
        size = jnp.where(p < x, between(chips, p, x), zero)
        put(XPRE + i, size, turned_by(chip_turn[:nx], x - 1 - p))
    for i, p in enumerate([x, *partners(x, nx)]):
        put(XTOT + i, between(chips, p, nx), turned_by(chip_turn[:nx], nx - 1 - p))
    put(XIN, between(chips, -1, x), turned_by(chip_turn[:nx], x))
    for i, p in enumerate(partners(y, ny)):
        size = jnp.where(p < y, between(line, p, y), zero)
        put(YPRE + i, size, turned_by(row_turn[:ny], y - 1 - p))
    put(YIN, between(line, -1, y), turned_by(row_turn[:ny], y))

    def select(flag, new, old):
        return tuple(jnp.where(flag, a, b) for a, b in zip(new, old))

    def pairwise(index, values, turns, place):
        unit, nothing = (one, zero), (zero, zero)
        late = lax.rem(index, 2) == 1
        rates = [(value * turns[1][0], value * turns[1][1]) for value in values]
        upper = rates[1]
        if len(values) == 4:
            upper = select(index >= 2, rates[3], rates[1])
        steps = [(select(late, upper, unit), select(late, unit, upper), select(late, unit, nothing))]
        if len(values) == 4:
            late = index >= 2
            block = values[2] * values[3]
            block = (block * turns[2][0], block * turns[2][1])
            before = select(index == 3, rates[2], select(index == 2, unit, nothing))
            steps.append((select(late, block, unit), select(late, unit, block), before))
        for i, factor in enumerate(f for step in steps for f in step):
            put(place + i, one, factor)

    pairwise(x, chips, chip_turn, XPAIR)
    pairwise(y, line, row_turn, YPAIR)


def mix_columns(left, middle, right, width):
    count = left.shape[0]
    column = lax.broadcasted_iota(jnp.int32, (count, 1), 0) % width
    left = jnp.where(column == 0, 0.0, pltpu.roll(left, 1, 0))
    right = jnp.where(column == width - 1, 0.0, pltpu.roll(right, count - 1, 0))
    return middle + left + right


def taps_of(inputs, weight, taps, width):
    lhs = jnp.concatenate(inputs, axis=1)
    parts = [
        jnp.dot(
            lhs,
            jnp.concatenate([weight[a, b] for a in taps], axis=0),
            preferred_element_type=F32,
        )
        for b in range(3)
    ]
    return mix_columns(*parts, width)


def flat(value):
    return value.reshape(value.shape[0] * value.shape[1], value.shape[2])


def turned(tab, index, value):
    pairs = value.shape[-1] // 2
    re, im = tab[index, :, :pairs], tab[index, :, pairs:]
    v_re, v_im = value[..., :pairs], value[..., pairs:]
    return jnp.concatenate([re * v_re - im * v_im, im * v_re + re * v_im], axis=-1)


def tiles(value):
    return value.astype(F32).reshape(-1, 8, value.shape[-1])


def scan(update, tab, local, row, width):
    nf, chans = local.shape[1], local.shape[3]
    running = None
    for t in range(nf):
        new = tiles(update[t * width : (t + 1) * width])
        running = new if running is None else turned(tab, RATE + t, running) + new
        local[row, t] = running.reshape(width, chans)
    return running.reshape(width, chans)


def share(ends, keep, send):
    c = lax.axis_index(TM[2])
    keep[...] = jnp.where(c == 0, ends[0], ends[1])
    send[...] = jnp.where(c == 0, ends[1], ends[0])


def update_inner(x, w, mod_far, ang_far, local, keep, send, tab, mod, ang, sems, *, nx, ny):
    nf, rows, width, _ = x.shape
    copies = [
        pltpu.make_async_copy(mod_far, mod, sems.at[0]),
        pltpu.make_async_copy(ang_far, ang, sems.at[1]),
    ]
    for copy in copies:
        copy.start()
    updates = [
        taps_of([flat(x[:, r + a - 1]) for a in range(3)], w, range(3), width)
        for r in range(1, rows - 1)
    ]
    for copy in copies:
        copy.wait()
    fill_table(mod, ang, tab, nx, ny, nf)
    share([scan(update, tab, local, i, width) for i, update in enumerate(updates)], keep, send)


def update_outer(x, w, acc):
    _, rows, width, _ = x.shape
    acc[0] = taps_of([flat(x[:, 0]), flat(x[:, 1])], w, [1, 2], width)
    acc[1] = taps_of([flat(x[:, rows - 2]), flat(x[:, rows - 1])], w, [0, 1], width)


def finish_outer(acc, low, high, w, tab, local, keep, send, top, bottom):
    width = low.shape[1]
    z, zs = lax.axis_index("row"), lax.axis_size("row")
    first = taps_of([flat(low[...])], w, [0], width)
    last = taps_of([flat(high[...])], w, [2], width)
    ends = [
        scan(acc[0] + jnp.where(z > 0, first, 0.0), tab, local, 0, width),
        scan(acc[1] + jnp.where(z < zs - 1, last, 0.0), tab, local, 1, width),
    ]
    share(ends, keep, send)
    top[...] = local[0].astype(BF16)
    bottom[...] = local[1].astype(BF16)


def join_cores(keep, got, tab, start, *chip):
    c = lax.axis_index(TM[2])
    early = jnp.where(c == 0, keep[...], got[...])
    late = jnp.where(c == 0, got[...], keep[...])
    start[...] = early
    total = turned(tab, CORE + 1, tiles(early)) + tiles(late)
    for ref in chip:
        ref[...] = total.reshape(early.shape).astype(ref.dtype)


def join_pair(own, got, *refs, place, first):
    tab, prefix, total, message = refs[-4:]
    part = tiles(got[...])
    whole = turned(tab, place, part) + turned(tab, place + 1, tiles(own[...]))
    before = turned(tab, place + 2, part)
    if not first:
        before = before + tiles(refs[0][...])
    prefix[...] = before.reshape(prefix.shape)
    total[...] = whole.reshape(total.shape)
    message[...] = whole.reshape(total.shape).astype(BF16)


def join_row(*refs):
    own, *got, tab, prefix, total = refs
    before = whole = None
    for d, ref in enumerate((own, *got)):
        part = tiles(ref[...])
        term = turned(tab, XTOT + d, part)
        whole = term if whole is None else whole + term
        if d > 0:
            term = turned(tab, XPRE + d - 1, part)
            before = term if before is None else before + term
    prefix[...] = before.reshape(own.shape)
    total[...] = whole.reshape(own.shape).astype(BF16)


def entry_of(before, prefix, start, state_in, tab, rows):
    c = lax.axis_index(TM[2])
    entry = jnp.where(c == 0, state_in[rows[0]], state_in[rows[1]])
    total = turned(tab, YIN, tiles(entry)) + before
    chip = turned(tab, XIN, total) + tiles(prefix[...])
    other = turned(tab, CORE, chip) + tiles(start[...])
    chip, other = chip.reshape(prefix.shape), other.reshape(prefix.shape)
    return jnp.where(c == 0, chip, other), jnp.where(c == 0, other, chip)


def join_inner(got, *refs, place):
    *earlier, prefix, start, state_in, tab, keep, send = refs
    before = turned(tab, place + 2, tiles(got[...]))
    for ref in earlier:
        before = before + tiles(ref[...])
    keep[...], send[...] = entry_of(before, prefix, start, state_in, tab, (1, 2))


def join_outer(*refs):
    *got, prefix, start, state_in, tab, send_in, keep, send, both = refs
    before = None
    for d, ref in enumerate(got):
        term = turned(tab, YPRE + d, tiles(ref[...]))
        before = term if before is None else before + term
    keep[...], send[...] = entry_of(before, prefix, start, state_in, tab, (0, 3))
    both[0] = send_in[...]
    both[1] = send[...]


def states(local, entry, tab):
    nf, width, chans = local.shape
    entry = tiles(entry)
    return jnp.concatenate(
        [
            (tiles(local[t]) + turned(tab, PROD + t, entry)).reshape(width, chans).astype(BF16)
            for t in range(nf)
        ],
        axis=0,
    )


def gelu(v):
    return 0.5 * v * (1.0 + lax.erf(v * (0.5**0.5)))


def conv_state(
    inner, outer, keep_in, keep_out, got, tab, w, acc_top, acc_bottom, out
):
    _, nf, width, chans = inner.shape
    rows = 4
    c = lax.axis_index(TM[2])
    row = []
    for local, i, keep, group in (
        (outer, 0, keep_out, 1),
        (inner, 0, keep_in, 0),
        (inner, 1, keep_in, 0),
        (outer, 1, keep_out, 1),
    ):
        row.append(states(local[i], jnp.where(c == i, keep[...], got[group]), tab))
    for r in list(range(1, rows - 1)) + [0, rows - 1]:
        taps = [a for a in range(3) if 0 <= r + a - 1 < rows]
        result = taps_of([row[r + a - 1] for a in taps], w, taps, width)
        if r == 0:
            acc_top[...] = result
        elif r == rows - 1:
            acc_bottom[...] = result
        else:
            out[r - 1] = gelu(result).reshape(nf, width, chans).astype(BF16)


def finish_output(
    acc_top, acc_bottom, low, high, same, cross, tab, w, inside, out, edge, sems
):
    nf, width, chans = low.shape
    rows = inside.shape[0] + 2
    z, zs = lax.axis_index("row"), lax.axis_size("row")
    c = lax.axis_index(TM[2])
    copies = []
    for r in range(1, rows - 1):
        copies.append(pltpu.make_async_copy(inside.at[r - 1], out.at[:, r], sems.at[r]))
        copies[-1].start()
    for i, (acc, halo, entry, tap, live, r) in enumerate(
        [
            (acc_top, low, jnp.where(c == 0, cross[...], same[...]), 0, z > 0, 0),
            (acc_bottom, high, jnp.where(c == 0, same[...], cross[...]), 2, z < zs - 1, rows - 1),
        ]
    ):
        part = taps_of([states(halo[...], entry, tab)], w, [tap], width)
        total = acc[...] + jnp.where(live, part, 0.0)
        edge[i] = gelu(total).reshape(nf, width, chans).astype(BF16)
        copies.append(pltpu.make_async_copy(edge.at[i], out.at[:, r], sems.at[r]))
        copies[-1].start()
    for copy in copies:
        copy.wait()


def swap(value):
    return lax.ppermute(value, TM[2], [(0, 1), (1, 0)])


def shift(value, distance):
    count = lax.axis_size("row")
    return lax.ppermute(
        value, "row", [(i, i + distance) for i in range(count) if 0 <= i + distance < count]
    )


def others(value, axis):
    count = lax.axis_size(axis)
    pairs = [[(i, p) for i, p in enumerate(group)] for group in zip(*(
        [int(p) for p in host_partners(i, count)] for i in range(count)
    ))]
    return [lax.ppermute(value, axis, pair) for pair in pairs]


def host_partners(index, count):
    if count == 2:
        return [1 - index]
    return [(index + 2) % 4, index ^ 1, 3 - index]


def shards(frames, state_in, modulus, angle, w_in, w_out):
    nf, rows, width, chans = frames.shape
    ny, nx, _ = (lax.axis_size(name) for name in TM)
    zs = lax.axis_size("row")
    far, modulus = (pltpu.with_memory_space_constraint(v, pltpu.HBM) for v in (frames, modulus))
    angle = pltpu.with_memory_space_constraint(angle[None], pltpu.HBM)
    conv_flops = 2 * nf * rows * width * 9 * chans * chans
    conv_bytes = 9 * chans * chans * 2

    def shape(*dims, dtype=F32):
        return jax.ShapeDtypeStruct(dims, dtype)

    row_bf = shape(nf, width, chans, dtype=BF16)
    acc_row = shape(nf * width, chans)
    one_row = shape(width, chans)
    one_bf = shape(width, chans, dtype=BF16)
    two_rows = shape(2, nf, width, chans)

    first, last = call(
        edges,
        (row_bf, row_bf),
        [HBM],
        scratch=[pltpu.SemaphoreType.DMA((2,))],
        flops=conv_flops * 10,
        size=20 * conv_bytes,
    )(far)
    low = shift(last, 1)
    high = shift(first, -1)

    def pair_steps(own, message, axis, place, keep_last):
        count = lax.axis_size(axis)
        partner = [lambda i: i ^ 1, lambda i: 3 - i][: 1 if count == 2 else 2]
        prefix = []
        for i, of in enumerate(partner):
            got = lax.ppermute(message, axis, [(k, of(k)) for k in range(count)])
            if keep_last and i == len(partner) - 1:
                return got, prefix, place + 3 * i
            before, own, message = call(
                functools.partial(join_pair, place=place + 3 * i, first=i == 0),
                (one_row, one_row, one_bf),
                [VM] * (3 + len(prefix)),
            )(own, got, *prefix, tab)
            prefix = [before]
        return own, message, before

    inner, keep, send, tab = call(
        functools.partial(update_inner, nx=nx, ny=ny),
        (two_rows, one_row, one_row, shape(ROWS, 8, chans)),
        [VM, VM, HBM, HBM],
        scratch=[
            pltpu.VMEM(modulus.shape, F32),
            pltpu.VMEM(angle.shape, F32),
            pltpu.SemaphoreType.DMA((2,)),
        ],
        flops=conv_flops // 2,
        size=conv_bytes,
    )(frames, w_in, modulus, angle)
    got = swap(send)
    acc = call(
        update_outer,
        shape(2, nf * width, chans),
        [VM, VM],
        flops=conv_flops // 3,
        size=conv_bytes,
    )(frames, w_in)
    start, own, message = call(join_cores, (one_row, one_row, one_bf), [VM] * 3)(keep, got, tab)
    own, message, prefix = pair_steps(own, message, TM[1], XPAIR, False)
    got, before, place = pair_steps(own, message, TM[0], YPAIR, True)
    keep_in, send_in = call(
        functools.partial(join_inner, place=place), (one_row, one_row), [VM] * (5 + len(before))
    )(got, *before, prefix, start, state_in, tab)

    outer, keep, send, top, bottom = call(
        finish_outer,
        (two_rows, one_row, one_row, row_bf, row_bf),
        [VM] * 5,
        flops=conv_flops // 6,
        size=conv_bytes,
    )(acc, low, high, w_in, tab)
    got = swap(send)
    low = shift(bottom, 1)
    high = shift(top, -1)
    start, chip = call(join_cores, (one_row, one_bf), [VM] * 3)(keep, got, tab)
    across = others(chip, TM[1])
    prefix, total = call(join_row, (one_row, one_bf), [VM] * (nx + 1))(chip, *across, tab)
    across = others(total, TM[0])
    keep_out, send, both = call(
        join_outer, (one_row, one_row, shape(2, width, chans)), [VM] * (ny + 4)
    )(*across, prefix, start, state_in, tab, send_in)
    got = swap(both)
    step = [-1, 1]
    same, cross = (
        lax.ppermute(
            value,
            (TM[2], "row"),
            [
                (c * zs + z, (c ^ flip) * zs + z + step[c])
                for c in range(2)
                for z in range(zs)
                if 0 <= z + step[c] < zs
            ],
        )
        for value, flip in ((keep_out, 0), (send, 1))
    )
    acc_top, acc_bottom, inside = call(
        conv_state,
        (acc_row, acc_row, shape(rows - 2, nf, width, chans, dtype=BF16)),
        [VM] * 7,
        flops=conv_flops * 10 // 12,
        size=conv_bytes,
    )(inner, outer, keep_in, keep_out, got, tab, w_out)
    return call(
        finish_output,
        shape(nf, rows, width, chans, dtype=BF16),
        [VM] * 9,
        out_specs=HBM,
        scratch=[pltpu.VMEM((2, nf, width, chans), BF16), pltpu.SemaphoreType.DMA((rows,))],
        flops=conv_flops // 6,
        size=conv_bytes,
    )(acc_top, acc_bottom, low, high, same, cross, tab, w_out, inside)


def solution(mesh):
    chips = mesh.shape["tm"] // 2
    side = int(chips**0.5)
    finer = Mesh(
        mesh.devices.reshape(chips // side, side, 2, mesh.shape["row"]), (*TM, "row")
    )
    placed = (P(TM, "row", None, None), P("row", None, None), P(), P(), P(), P())

    return jax.shard_map(
        shards, mesh=finer, in_specs=placed, out_specs=P(TM, "row", None, None), check_vma=False
    )
```

```python
import functools

import jax
import jax.numpy as jnp
from jax import lax
from jax.experimental import pallas as pl
from jax.experimental.pallas import tpu as pltpu
from jax.sharding import Mesh
from jax.sharding import PartitionSpec as P

TM = ("tm_0", "tm_1", "tm_2")
F32 = jnp.float32
BF16 = jnp.bfloat16
VM = pl.BlockSpec(memory_space=pltpu.VMEM)
HBM = pl.BlockSpec(memory_space=pltpu.HBM)

RATE, PROD, CORE, XPRE, XTOT, XIN, YPRE, YIN, XPAIR, YPAIR, ROWS = 0, 4, 8, 10, 13, 17, 18, 21, 22, 28, 34


def call(kernel, outs, specs, out_specs=None, scratch=(), flops=0, size=0, limit=24, aliases=None):
    return pl.pallas_call(
        kernel,
        out_shape=outs,
        in_specs=specs,
        out_specs=out_specs if out_specs is not None else jax.tree.map(lambda _: VM, outs),
        scratch_shapes=list(scratch),
        input_output_aliases=aliases or {},
        cost_estimate=pl.CostEstimate(flops=flops, bytes_accessed=size, transcendentals=0),
        compiler_params=pltpu.CompilerParams(vmem_limit_bytes=limit << 20),
    )


def cmul(a, b):
    return (a[0] * b[0] - a[1] * b[1], a[0] * b[1] + a[1] * b[0])


def partners(index, count):
    if count == 2:
        return [1 - index]
    return [lax.rem(index + 2, 4), index + 1 - 2 * lax.rem(index, 2), 3 - index]


def powers(base, count):
    out = [(jnp.ones_like(base[0]), jnp.zeros_like(base[0]))]
    for _ in range(count):
        out.append(cmul(out[-1], base))
    return out


def edges(frames, inward, outward, sems):
    rows = frames.shape[1]
    c = lax.axis_index(TM[2])
    copies = [
        pltpu.make_async_copy(frames.at[:, (1 - c) * (rows - 1)], inward, sems.at[0]),
        pltpu.make_async_copy(frames.at[:, c * (rows - 1)], outward, sems.at[1]),
    ]
    for copy in copies:
        copy.start()
    for copy in copies:
        copy.wait()


def fill_table(mod, ang, tab, nx, ny, nf):
    y, x, c = (lax.axis_index(name) for name in TM)
    pairs = mod.shape[1]
    shape = (8, pairs)
    theta = jnp.broadcast_to(ang[...], shape)
    turn = (jnp.cos(theta), jnp.sin(theta))
    local = powers(turn, nf)
    chip_turn = powers(cmul(local[nf], local[nf]), nx)
    row_turn = powers(chip_turn[nx], ny)

    def put(index, size, angle):
        tab[index, :, :pairs] = size * angle[0]
        tab[index, :, pairs:] = size * angle[1]

    def product8(v):
        v = v * pltpu.roll(v, 7, 0)
        v = v * pltpu.roll(v, 6, 0)
        return v * pltpu.roll(v, 4, 0)

    def chip_rows(index):
        return mod[pl.ds(pl.multiple_of(index * 8, 8), 8), :]

    one = jnp.ones(shape, F32)
    zero = jnp.zeros(shape, F32)
    mine = chip_rows(y * nx + x)
    ms = [jnp.broadcast_to(mine[i : i + 1], shape) for i in range(2 * nf)]
    running = None
    for t in range(nf):
        m = jnp.where(c == 0, ms[t], ms[nf + t])
        running = m if running is None else running * m
        put(RATE + t, m, turn)
        put(PROD + t, running, local[t + 1])
    for core in range(2):
        total = ms[core * nf]
        for t in range(1, nf):
            total = total * ms[core * nf + t]
        put(CORE + core, total, local[nf])
    chips = [product8(chip_rows(y * nx + u)) for u in range(nx)]
    line = []
    for v in range(ny):
        total = product8(chip_rows(v * nx))
        for u in range(1, nx):
            total = total * product8(chip_rows(v * nx + u))
        line.append(total)

    def between(values, low, high):
        total = one
        for u, value in enumerate(values):
            total = total * jnp.where((u > low) & (u < high), value, one)
        return total

    def turned_by(turns, count):
        angle = turns[0]
        for k in range(1, len(turns)):
            angle = tuple(jnp.where(count == k, new, old) for new, old in zip(turns[k], angle))
        return angle

    for i, p in enumerate(partners(x, nx)):
        size = jnp.where(p < x, between(chips, p, x), zero)
        put(XPRE + i, size, turned_by(chip_turn[:nx], x - 1 - p))
    for i, p in enumerate([x, *partners(x, nx)]):
        put(XTOT + i, between(chips, p, nx), turned_by(chip_turn[:nx], nx - 1 - p))
    put(XIN, between(chips, -1, x), turned_by(chip_turn[:nx], x))
    for i, p in enumerate(partners(y, ny)):
        size = jnp.where(p < y, between(line, p, y), zero)
        put(YPRE + i, size, turned_by(row_turn[:ny], y - 1 - p))
    put(YIN, between(line, -1, y), turned_by(row_turn[:ny], y))

    def select(flag, new, old):
        return tuple(jnp.where(flag, a, b) for a, b in zip(new, old))

    def pairwise(index, values, turns, place):
        unit, nothing = (one, zero), (zero, zero)
        late = lax.rem(index, 2) == 1
        rates = [(value * turns[1][0], value * turns[1][1]) for value in values]
        upper = rates[1]
        if len(values) == 4:
            upper = select(index >= 2, rates[3], rates[1])
        steps = [(select(late, upper, unit), select(late, unit, upper), select(late, unit, nothing))]
        if len(values) == 4:
            late = index >= 2
            block = values[2] * values[3]
            block = (block * turns[2][0], block * turns[2][1])
            before = select(index == 3, rates[2], select(index == 2, unit, nothing))
            steps.append((select(late, block, unit), select(late, unit, block), before))
        for i, factor in enumerate(f for step in steps for f in step):
            put(place + i, one, factor)

    pairwise(x, chips, chip_turn, XPAIR)
    pairwise(y, line, row_turn, YPAIR)


def mix_columns(left, middle, right, width):
    count = left.shape[0]
    column = lax.broadcasted_iota(jnp.int32, (count, 1), 0) % width
    left = jnp.where(column == 0, 0.0, pltpu.roll(left, 1, 0))
    right = jnp.where(column == width - 1, 0.0, pltpu.roll(right, count - 1, 0))
    return middle + left + right


def taps_of(inputs, weight, taps, width):
    lhs = jnp.concatenate(inputs, axis=1)
    parts = [
        jnp.dot(
            lhs,
            jnp.concatenate([weight[a, b] for a in taps], axis=0),
            preferred_element_type=F32,
        )
        for b in range(3)
    ]
    return mix_columns(*parts, width)


def flat(value):
    return value.reshape(value.shape[0] * value.shape[1], value.shape[2])


def turned(tab, index, value):
    pairs = value.shape[-1] // 2
    re, im = tab[index, :, :pairs], tab[index, :, pairs:]
    v_re, v_im = value[..., :pairs], value[..., pairs:]
    return jnp.concatenate([re * v_re - im * v_im, im * v_re + re * v_im], axis=-1)


def tiles(value):
    return value.astype(F32).reshape(-1, 8, value.shape[-1])


def scan(update, tab, local, row, width):
    nf, chans = local.shape[1], local.shape[3]
    running = None
    for t in range(nf):
        new = tiles(update[t * width : (t + 1) * width])
        running = new if running is None else turned(tab, RATE + t, running) + new
        local[row, t] = running.reshape(width, chans)
    return running.reshape(width, chans)


def share(ends, keep, send):
    c = lax.axis_index(TM[2])
    keep[...] = jnp.where(c == 0, ends[0], ends[1])
    send[...] = jnp.where(c == 0, ends[1], ends[0])


def update_inner(x, w, mod_far, ang_far, local, keep, send, tab, mod, ang, sems, *, nx, ny):
    nf, rows, width, _ = x.shape
    copies = [
        pltpu.make_async_copy(mod_far, mod, sems.at[0]),
        pltpu.make_async_copy(ang_far, ang, sems.at[1]),
    ]
    for copy in copies:
        copy.start()
    updates = [
        taps_of([flat(x[:, r + a - 1]) for a in range(3)], w, range(3), width)
        for r in range(1, rows - 1)
    ]
    for copy in copies:
        copy.wait()
    fill_table(mod, ang, tab, nx, ny, nf)
    share([scan(update, tab, local, i, width) for i, update in enumerate(updates)], keep, send)


def update_outer(x, w, acc):
    _, rows, width, _ = x.shape
    acc[0] = taps_of([flat(x[:, 0]), flat(x[:, 1])], w, [1, 2], width)
    acc[1] = taps_of([flat(x[:, rows - 2]), flat(x[:, rows - 1])], w, [0, 1], width)


def in_order(first, second):
    c = lax.axis_index(TM[2])
    return jnp.where(c == 0, first, second), jnp.where(c == 0, second, first)


def finish_outer(acc, got_one, got_two, w, tab, local, keep, send, one, two):
    width = got_one.shape[1]
    c = lax.axis_index(TM[2])
    low, high = in_order(got_one[...], got_two[...])
    z, zs = lax.axis_index("row"), lax.axis_size("row")
    first = taps_of([flat(low)], w, [0], width)
    last = taps_of([flat(high)], w, [2], width)
    ends = [
        scan(acc[0] + jnp.where(z > 0, first, 0.0), tab, local, 0, width),
        scan(acc[1] + jnp.where(z < zs - 1, last, 0.0), tab, local, 1, width),
    ]
    share(ends, keep, send)
    one[...] = jnp.where(c == 0, local[1], local[0]).astype(BF16)
    two[...] = jnp.where(c == 0, local[0], local[1]).astype(BF16)


def join_cores(keep, got, tab, start, *chip):
    c = lax.axis_index(TM[2])
    early = jnp.where(c == 0, keep[...], got[...])
    late = jnp.where(c == 0, got[...], keep[...])
    start[...] = early
    total = turned(tab, CORE + 1, tiles(early)) + tiles(late)
    for ref in chip:
        ref[...] = total.reshape(early.shape).astype(ref.dtype)


def join_pair(own, got, *refs, place, first):
    tab, prefix, total, message = refs[-4:]
    part = tiles(got[...])
    whole = turned(tab, place, part) + turned(tab, place + 1, tiles(own[...]))
    before = turned(tab, place + 2, part)
    if not first:
        before = before + tiles(refs[0][...])
    prefix[...] = before.reshape(prefix.shape)
    total[...] = whole.reshape(total.shape)
    message[...] = whole.reshape(total.shape).astype(BF16)


def join_row(*refs):
    own, *got, tab, prefix, total = refs
    before = whole = None
    for d, ref in enumerate((own, *got)):
        part = tiles(ref[...])
        term = turned(tab, XTOT + d, part)
        whole = term if whole is None else whole + term
        if d > 0:
            term = turned(tab, XPRE + d - 1, part)
            before = term if before is None else before + term
    prefix[...] = before.reshape(own.shape)
    total[...] = whole.reshape(own.shape).astype(BF16)


def entry_of(before, prefix, start, state_in, tab, rows):
    c = lax.axis_index(TM[2])
    entry = jnp.where(c == 0, state_in[rows[0]], state_in[rows[1]])
    total = turned(tab, YIN, tiles(entry)) + before
    chip = turned(tab, XIN, total) + tiles(prefix[...])
    other = turned(tab, CORE, chip) + tiles(start[...])
    chip, other = chip.reshape(prefix.shape), other.reshape(prefix.shape)
    return jnp.where(c == 0, chip, other), jnp.where(c == 0, other, chip)


def join_inner(got, *refs, place):
    *earlier, prefix, start, state_in, tab, keep, send = refs
    before = turned(tab, place + 2, tiles(got[...]))
    for ref in earlier:
        before = before + tiles(ref[...])
    keep[...], send[...] = entry_of(before, prefix, start, state_in, tab, (1, 2))


def join_outer(*refs):
    *got, prefix, start, state_in, tab, keep, send = refs
    before = None
    for d, ref in enumerate(got):
        term = turned(tab, YPRE + d, tiles(ref[...]))
        before = term if before is None else before + term
    keep[...], send[...] = entry_of(before, prefix, start, state_in, tab, (0, 3))


def states(local, entry, tab):
    nf, width, chans = local.shape
    entry = tiles(entry)
    return jnp.concatenate(
        [
            (tiles(local[t]) + turned(tab, PROD + t, entry)).reshape(width, chans).astype(BF16)
            for t in range(nf)
        ],
        axis=0,
    )


def gelu(v):
    return 0.5 * v * (1.0 + lax.erf(v * (0.5**0.5)))


def conv_state(
    inner, outer, keep_in, got_in, keep_out, got_out, tab, w, acc_top, acc_bottom, out
):
    _, nf, width, chans = inner.shape
    rows = 4
    c = lax.axis_index(TM[2])
    row = []
    for local, i, keep, got in (
        (outer, 0, keep_out, got_out),
        (inner, 0, keep_in, got_in),
        (inner, 1, keep_in, got_in),
        (outer, 1, keep_out, got_out),
    ):
        row.append(states(local[i], jnp.where(c == i, keep[...], got[...]), tab))
    for r in list(range(1, rows - 1)) + [0, rows - 1]:
        taps = [a for a in range(3) if 0 <= r + a - 1 < rows]
        result = taps_of([row[r + a - 1] for a in taps], w, taps, width)
        if r == 0:
            acc_top[...] = result
        elif r == rows - 1:
            acc_bottom[...] = result
        else:
            out[r - 1] = gelu(result).reshape(nf, width, chans).astype(BF16)


def finish_output(
    acc_top, acc_bottom, one, two, entry_one, entry_two, tab, w, inside, out, edge, sems
):
    nf, width, chans = one.shape
    rows = inside.shape[0] + 2
    z, zs = lax.axis_index("row"), lax.axis_size("row")
    low, high = in_order(one[...], two[...])
    entry_low, entry_high = in_order(entry_one[...], entry_two[...])
    copies = []
    for r in range(1, rows - 1):
        copies.append(pltpu.make_async_copy(inside.at[r - 1], out.at[:, r], sems.at[r]))
        copies[-1].start()
    for i, (acc, halo, entry, tap, live, r) in enumerate(
        [
            (acc_top, low, entry_low, 0, z > 0, 0),
            (acc_bottom, high, entry_high, 2, z < zs - 1, rows - 1),
        ]
    ):
        part = taps_of([states(halo, entry, tab)], w, [tap], width)
        total = acc[...] + jnp.where(live, part, 0.0)
        edge[i] = gelu(total).reshape(nf, width, chans).astype(BF16)
        copies.append(pltpu.make_async_copy(edge.at[i], out.at[:, r], sems.at[r]))
        copies[-1].start()
    for copy in copies:
        copy.wait()


def swap(value):
    return lax.ppermute(value, TM[2], [(0, 1), (1, 0)])


def shift(value, sign):
    count = lax.axis_size("row")
    pairs = []
    for c, step in ((0, sign), (1, -sign)):
        for z in range(count):
            inside = 0 <= z + step < count
            pairs.append((c * count + z, c * count + z + step if inside else (1 - c) * count + z))
    return lax.ppermute(value, (TM[2], "row"), pairs)


def others(value, axis):
    count = lax.axis_size(axis)
    pairs = [[(i, p) for i, p in enumerate(group)] for group in zip(*(
        [int(p) for p in host_partners(i, count)] for i in range(count)
    ))]
    return [lax.ppermute(value, axis, pair) for pair in pairs]


def host_partners(index, count):
    if count == 2:
        return [1 - index]
    return [(index + 2) % 4, index ^ 1, 3 - index]


def shards(frames, state_in, modulus, angle, w_in, w_out):
    nf, rows, width, chans = frames.shape
    ny, nx, _ = (lax.axis_size(name) for name in TM)
    far, modulus = (pltpu.with_memory_space_constraint(v, pltpu.HBM) for v in (frames, modulus))
    angle = pltpu.with_memory_space_constraint(angle[None], pltpu.HBM)
    conv_flops = 2 * nf * rows * width * 9 * chans * chans
    conv_bytes = 9 * chans * chans * 2

    def shape(*dims, dtype=F32):
        return jax.ShapeDtypeStruct(dims, dtype)

    row_bf = shape(nf, width, chans, dtype=BF16)
    acc_row = shape(nf * width, chans)
    one_row = shape(width, chans)
    one_bf = shape(width, chans, dtype=BF16)
    two_rows = shape(2, nf, width, chans)

    one, two = call(
        edges,
        (row_bf, row_bf),
        [HBM],
        scratch=[pltpu.SemaphoreType.DMA((2,))],
        flops=conv_flops * 10,
        size=20 * conv_bytes,
    )(far)
    got_one, got_two = shift(one, 1), shift(two, -1)

    def pair_steps(own, message, axis, place, keep_last):
        count = lax.axis_size(axis)
        partner = [lambda i: i ^ 1, lambda i: 3 - i][: 1 if count == 2 else 2]
        prefix = []
        for i, of in enumerate(partner):
            got = lax.ppermute(message, axis, [(k, of(k)) for k in range(count)])
            if keep_last and i == len(partner) - 1:
                return got, prefix, place + 3 * i
            before, own, message = call(
                functools.partial(join_pair, place=place + 3 * i, first=i == 0),
                (one_row, one_row, one_bf),
                [VM] * (3 + len(prefix)),
            )(own, got, *prefix, tab)
            prefix = [before]
        return own, message, before

    inner, keep, send, tab = call(
        functools.partial(update_inner, nx=nx, ny=ny),
        (two_rows, one_row, one_row, shape(ROWS, 8, chans)),
        [VM, VM, HBM, HBM],
        scratch=[
            pltpu.VMEM(modulus.shape, F32),
            pltpu.VMEM(angle.shape, F32),
            pltpu.SemaphoreType.DMA((2,)),
        ],
        flops=conv_flops // 2,
        size=conv_bytes,
    )(frames, w_in, modulus, angle)
    got = swap(send)
    acc = call(
        update_outer,
        shape(2, nf * width, chans),
        [VM, VM],
        flops=conv_flops // 3,
        size=conv_bytes,
    )(frames, w_in)
    start, own, message = call(join_cores, (one_row, one_row, one_bf), [VM] * 3)(keep, got, tab)
    own, message, prefix = pair_steps(own, message, TM[1], XPAIR, False)
    got, before, place = pair_steps(own, message, TM[0], YPAIR, True)
    keep_in, send_in = call(
        functools.partial(join_inner, place=place), (one_row, one_row), [VM] * (5 + len(before))
    )(got, *before, prefix, start, state_in, tab)
    got_in = swap(send_in)

    outer, keep, send, one, two = call(
        finish_outer,
        (two_rows, one_row, one_row, row_bf, row_bf),
        [VM] * 5,
        flops=conv_flops // 6,
        size=conv_bytes,
    )(acc, got_one, got_two, w_in, tab)
    got = swap(send)
    got_one, got_two = shift(one, 1), shift(two, -1)
    start, chip = call(join_cores, (one_row, one_bf), [VM] * 3)(keep, got, tab)
    across = others(chip, TM[1])
    prefix, total = call(join_row, (one_row, one_bf), [VM] * (nx + 1))(chip, *across, tab)
    across = others(total, TM[0])
    keep_out, send = call(join_outer, (one_row, one_row), [VM] * (ny + 3))(
        *across, prefix, start, state_in, tab
    )
    got_out = swap(send)
    entry_two = shift(keep_out, -1)
    entry_one = shift(got_out, 1)
    acc_top, acc_bottom, inside = call(
        conv_state,
        (acc_row, acc_row, shape(rows - 2, nf, width, chans, dtype=BF16)),
        [VM] * 8,
        flops=conv_flops * 10 // 12,
        size=conv_bytes,
    )(inner, outer, keep_in, got_in, keep_out, got_out, tab, w_out)
    return call(
        finish_output,
        shape(nf, rows, width, chans, dtype=BF16),
        [VM] * 9,
        out_specs=HBM,
        scratch=[pltpu.VMEM((2, nf, width, chans), BF16), pltpu.SemaphoreType.DMA((rows,))],
        flops=conv_flops // 6,
        size=conv_bytes,
    )(acc_top, acc_bottom, got_one, got_two, entry_one, entry_two, tab, w_out, inside)


def solution(mesh):
    chips = mesh.shape["tm"] // 2
    side = int(chips**0.5)
    finer = Mesh(
        mesh.devices.reshape(chips // side, side, 2, mesh.shape["row"]), (*TM, "row")
    )
    placed = (P(TM, "row", None, None), P("row", None, None), P(), P(), P(), P())

    return jax.shard_map(
        shards, mesh=finer, in_specs=placed, out_specs=P(TM, "row", None, None), check_vma=False
    )
```

```python
import functools

import jax
import jax.numpy as jnp
from jax import lax
from jax.experimental import pallas as pl
from jax.experimental.pallas import tpu as pltpu
from jax.sharding import Mesh
from jax.sharding import PartitionSpec as P

TM = ("tm_0", "tm_1", "tm_2")
F32 = jnp.float32
BF16 = jnp.bfloat16
VM = pl.BlockSpec(memory_space=pltpu.VMEM)
HBM = pl.BlockSpec(memory_space=pltpu.HBM)

RATE, PROD, CORE, XPRE, XTOT, XIN, YPRE, YIN, XPAIR, YPAIR, ROWS = 0, 4, 8, 10, 13, 17, 18, 21, 22, 28, 34


def call(kernel, outs, specs, out_specs=None, scratch=(), flops=0, size=0, limit=24, aliases=None):
    return pl.pallas_call(
        kernel,
        out_shape=outs,
        in_specs=specs,
        out_specs=out_specs if out_specs is not None else jax.tree.map(lambda _: VM, outs),
        scratch_shapes=list(scratch),
        input_output_aliases=aliases or {},
        cost_estimate=pl.CostEstimate(flops=flops, bytes_accessed=size, transcendentals=0),
        compiler_params=pltpu.CompilerParams(vmem_limit_bytes=limit << 20),
    )


def cmul(a, b):
    return (a[0] * b[0] - a[1] * b[1], a[0] * b[1] + a[1] * b[0])


def partners(index, count):
    if count == 2:
        return [1 - index]
    return [lax.rem(index + 2, 4), index + 1 - 2 * lax.rem(index, 2), 3 - index]


def powers(base, count):
    out = [(jnp.ones_like(base[0]), jnp.zeros_like(base[0]))]
    for _ in range(count):
        out.append(cmul(out[-1], base))
    return out


def edges(frames, inward, outward, sems):
    rows = frames.shape[1]
    c = lax.axis_index(TM[2])
    copies = [
        pltpu.make_async_copy(frames.at[:, (1 - c) * (rows - 1)], inward, sems.at[0]),
        pltpu.make_async_copy(frames.at[:, c * (rows - 1)], outward, sems.at[1]),
    ]
    for copy in copies:
        copy.start()
    for copy in copies:
        copy.wait()


def fill_table(mod, ang, tab, nx, ny, nf):
    y, x, c = (lax.axis_index(name) for name in TM)
    pairs = mod.shape[1]
    shape = (8, pairs)
    theta = jnp.broadcast_to(ang[...], shape)
    turn = (jnp.cos(theta), jnp.sin(theta))
    local = powers(turn, nf)
    chip_turn = powers(cmul(local[nf], local[nf]), nx)
    row_turn = powers(chip_turn[nx], ny)

    def put(index, size, angle):
        tab[index, :, :pairs] = size * angle[0]
        tab[index, :, pairs:] = size * angle[1]

    def product8(v):
        v = v * pltpu.roll(v, 7, 0)
        v = v * pltpu.roll(v, 6, 0)
        return v * pltpu.roll(v, 4, 0)

    def chip_rows(index):
        return mod[pl.ds(pl.multiple_of(index * 8, 8), 8), :]

    one = jnp.ones(shape, F32)
    zero = jnp.zeros(shape, F32)
    mine = chip_rows(y * nx + x)
    ms = [jnp.broadcast_to(mine[i : i + 1], shape) for i in range(2 * nf)]
    running = None
    for t in range(nf):
        m = jnp.where(c == 0, ms[t], ms[nf + t])
        running = m if running is None else running * m
        put(RATE + t, m, turn)
        put(PROD + t, running, local[t + 1])
    for core in range(2):
        total = ms[core * nf]
        for t in range(1, nf):
            total = total * ms[core * nf + t]
        put(CORE + core, total, local[nf])
    chips = [product8(chip_rows(y * nx + u)) for u in range(nx)]
    line = []
    for v in range(ny):
        total = product8(chip_rows(v * nx))
        for u in range(1, nx):
            total = total * product8(chip_rows(v * nx + u))
        line.append(total)

    def between(values, low, high):
        total = one
        for u, value in enumerate(values):
            total = total * jnp.where((u > low) & (u < high), value, one)
        return total

    def turned_by(turns, count):
        angle = turns[0]
        for k in range(1, len(turns)):
            angle = tuple(jnp.where(count == k, new, old) for new, old in zip(turns[k], angle))
        return angle

    for i, p in enumerate(partners(x, nx)):
        size = jnp.where(p < x, between(chips, p, x), zero)
        put(XPRE + i, size, turned_by(chip_turn[:nx], x - 1 - p))
    for i, p in enumerate([x, *partners(x, nx)]):
        put(XTOT + i, between(chips, p, nx), turned_by(chip_turn[:nx], nx - 1 - p))
    put(XIN, between(chips, -1, x), turned_by(chip_turn[:nx], x))
    for i, p in enumerate(partners(y, ny)):
        size = jnp.where(p < y, between(line, p, y), zero)
        put(YPRE + i, size, turned_by(row_turn[:ny], y - 1 - p))
    put(YIN, between(line, -1, y), turned_by(row_turn[:ny], y))

    def select(flag, new, old):
        return tuple(jnp.where(flag, a, b) for a, b in zip(new, old))

    def pairwise(index, values, turns, place):
        unit, nothing = (one, zero), (zero, zero)
        late = lax.rem(index, 2) == 1
        rates = [(value * turns[1][0], value * turns[1][1]) for value in values]
        upper = rates[1]
        if len(values) == 4:
            upper = select(index >= 2, rates[3], rates[1])
        steps = [(select(late, upper, unit), select(late, unit, upper), select(late, unit, nothing))]
        if len(values) == 4:
            late = index >= 2
            block = values[2] * values[3]
            block = (block * turns[2][0], block * turns[2][1])
            before = select(index == 3, rates[2], select(index == 2, unit, nothing))
            steps.append((select(late, block, unit), select(late, unit, block), before))
        for i, factor in enumerate(f for step in steps for f in step):
            put(place + i, one, factor)

    pairwise(x, chips, chip_turn, XPAIR)
    pairwise(y, line, row_turn, YPAIR)


def mix_columns(left, middle, right, width):
    count = left.shape[0]
    column = lax.broadcasted_iota(jnp.int32, (count, 1), 0) % width
    left = jnp.where(column == 0, 0.0, pltpu.roll(left, 1, 0))
    right = jnp.where(column == width - 1, 0.0, pltpu.roll(right, count - 1, 0))
    return middle + left + right


def taps_of(inputs, weight, taps, width):
    lhs = jnp.concatenate(inputs, axis=1)
    parts = [
        jnp.dot(
            lhs,
            jnp.concatenate([weight[a, b] for a in taps], axis=0),
            preferred_element_type=F32,
        )
        for b in range(3)
    ]
    return mix_columns(*parts, width)


def flat(value):
    return value.reshape(value.shape[0] * value.shape[1], value.shape[2])


def turned(tab, index, value):
    pairs = value.shape[-1] // 2
    re, im = tab[index, :, :pairs], tab[index, :, pairs:]
    v_re, v_im = value[..., :pairs], value[..., pairs:]
    return jnp.concatenate([re * v_re - im * v_im, im * v_re + re * v_im], axis=-1)


def tiles(value):
    return value.astype(F32).reshape(-1, 8, value.shape[-1])


def scan(update, tab, local, row, width):
    nf, chans = local.shape[1], local.shape[3]
    running = None
    for t in range(nf):
        new = tiles(update[t * width : (t + 1) * width])
        running = new if running is None else turned(tab, RATE + t, running) + new
        local[row, t] = running.reshape(width, chans)
    return running.reshape(width, chans)


def share(ends, keep, send):
    c = lax.axis_index(TM[2])
    keep[...] = jnp.where(c == 0, ends[0], ends[1])
    send[...] = jnp.where(c == 0, ends[1], ends[0])


def update_inner(x, w, mod_far, ang_far, local, keep, send, tab, mod, ang, sems, *, nx, ny):
    nf, rows, width, _ = x.shape
    copies = [
        pltpu.make_async_copy(mod_far, mod, sems.at[0]),
        pltpu.make_async_copy(ang_far, ang, sems.at[1]),
    ]
    for copy in copies:
        copy.start()
    updates = [
        taps_of([flat(x[:, r + a - 1]) for a in range(3)], w, range(3), width)
        for r in range(1, rows - 1)
    ]
    for copy in copies:
        copy.wait()
    fill_table(mod, ang, tab, nx, ny, nf)
    share([scan(update, tab, local, i, width) for i, update in enumerate(updates)], keep, send)


def update_outer(x, w, acc):
    _, rows, width, _ = x.shape
    acc[0] = taps_of([flat(x[:, 0]), flat(x[:, 1])], w, [1, 2], width)
    acc[1] = taps_of([flat(x[:, rows - 2]), flat(x[:, rows - 1])], w, [0, 1], width)


def in_order(first, second):
    c = lax.axis_index(TM[2])
    return jnp.where(c == 0, first, second), jnp.where(c == 0, second, first)


def finish_outer(acc, got_one, got_two, w, tab, local, keep, send, one, two):
    width = got_one.shape[1]
    c = lax.axis_index(TM[2])
    low, high = in_order(got_one[...], got_two[...])
    z, zs = lax.axis_index("row"), lax.axis_size("row")
    first = taps_of([flat(low)], w, [0], width)
    last = taps_of([flat(high)], w, [2], width)
    ends = [
        scan(acc[0] + jnp.where(z > 0, first, 0.0), tab, local, 0, width),
        scan(acc[1] + jnp.where(z < zs - 1, last, 0.0), tab, local, 1, width),
    ]
    share(ends, keep, send)
    one[...] = jnp.where(c == 0, local[1], local[0]).astype(BF16)
    two[...] = jnp.where(c == 0, local[0], local[1]).astype(BF16)


def join_cores(keep, got, tab, start, *chip):
    c = lax.axis_index(TM[2])
    early = jnp.where(c == 0, keep[...], got[...])
    late = jnp.where(c == 0, got[...], keep[...])
    start[...] = early
    total = turned(tab, CORE + 1, tiles(early)) + tiles(late)
    for ref in chip:
        ref[...] = total.reshape(early.shape).astype(ref.dtype)


def join_pair(own, got, *refs, place, first, goes_on):
    earlier, (tab, prefix, message, *total) = refs[: not first], refs[not first :]
    part = tiles(got[...])
    whole = turned(tab, place, part) + turned(tab, place + 1, tiles(own[...]))
    before = turned(tab, place + 2, part)
    for ref in earlier:
        before = before + tiles(ref[...])
    prefix[...] = before.reshape(prefix.shape)
    message[...] = whole.reshape(prefix.shape).astype(BF16)
    if goes_on:
        total[0][...] = whole.reshape(prefix.shape)


def join_row(*refs):
    own, *got, tab, prefix, total = refs
    before = whole = None
    for d, ref in enumerate((own, *got)):
        part = tiles(ref[...])
        term = turned(tab, XTOT + d, part)
        whole = term if whole is None else whole + term
        if d > 0:
            term = turned(tab, XPRE + d - 1, part)
            before = term if before is None else before + term
    prefix[...] = before.reshape(own.shape)
    total[...] = whole.reshape(own.shape).astype(BF16)


def entry_of(before, prefix, start, state_in, tab, rows):
    c = lax.axis_index(TM[2])
    entry = jnp.where(c == 0, state_in[rows[0]], state_in[rows[1]])
    total = turned(tab, YIN, tiles(entry)) + before
    chip = turned(tab, XIN, total) + tiles(prefix[...])
    other = turned(tab, CORE, chip) + tiles(start[...])
    chip, other = chip.reshape(prefix.shape), other.reshape(prefix.shape)
    return jnp.where(c == 0, chip, other), jnp.where(c == 0, other, chip)


def join_inner(got, *refs, place):
    *earlier, prefix, start, state_in, tab, keep, send = refs
    before = turned(tab, place + 2, tiles(got[...]))
    for ref in earlier:
        before = before + tiles(ref[...])
    keep[...], send[...] = entry_of(before, prefix, start, state_in, tab, (1, 2))


def join_outer(*refs):
    *got, prefix, start, state_in, tab, keep, send = refs
    before = None
    for d, ref in enumerate(got):
        term = turned(tab, YPRE + d, tiles(ref[...]))
        before = term if before is None else before + term
    keep[...], send[...] = entry_of(before, prefix, start, state_in, tab, (0, 3))


def states(local, entry, tab):
    nf, width, chans = local.shape
    entry = tiles(entry)
    return jnp.concatenate(
        [
            (tiles(local[t]) + turned(tab, PROD + t, entry)).reshape(width, chans).astype(BF16)
            for t in range(nf)
        ],
        axis=0,
    )


def gelu(v):
    return 0.5 * v * (1.0 + lax.erf(v * (0.5**0.5)))


def conv_state(
    inner, outer, keep_in, got_in, keep_out, got_out, tab, w, acc_top, acc_bottom, out
):
    _, nf, width, chans = inner.shape
    rows = 4
    c = lax.axis_index(TM[2])
    row = []
    for local, i, keep, got in (
        (outer, 0, keep_out, got_out),
        (inner, 0, keep_in, got_in),
        (inner, 1, keep_in, got_in),
        (outer, 1, keep_out, got_out),
    ):
        row.append(states(local[i], jnp.where(c == i, keep[...], got[...]), tab))
    for r in list(range(1, rows - 1)) + [0, rows - 1]:
        taps = [a for a in range(3) if 0 <= r + a - 1 < rows]
        result = taps_of([row[r + a - 1] for a in taps], w, taps, width)
        if r == 0:
            acc_top[...] = result
        elif r == rows - 1:
            acc_bottom[...] = result
        else:
            out[r - 1] = gelu(result).reshape(nf, width, chans).astype(BF16)


def finish_output(
    acc_top, acc_bottom, one, two, entry_one, entry_two, tab, w, inside, out, edge, sems
):
    nf, width, chans = one.shape
    rows = inside.shape[0] + 2
    z, zs = lax.axis_index("row"), lax.axis_size("row")
    low, high = in_order(one[...], two[...])
    entry_low, entry_high = in_order(entry_one[...], entry_two[...])
    copies = []
    for r in range(1, rows - 1):
        copies.append(pltpu.make_async_copy(inside.at[r - 1], out.at[:, r], sems.at[r]))
        copies[-1].start()
    for i, (acc, halo, entry, tap, live, r) in enumerate(
        [
            (acc_top, low, entry_low, 0, z > 0, 0),
            (acc_bottom, high, entry_high, 2, z < zs - 1, rows - 1),
        ]
    ):
        part = taps_of([states(halo, entry, tab)], w, [tap], width)
        total = acc[...] + jnp.where(live, part, 0.0)
        edge[i] = gelu(total).reshape(nf, width, chans).astype(BF16)
        copies.append(pltpu.make_async_copy(edge.at[i], out.at[:, r], sems.at[r]))
        copies[-1].start()
    for copy in copies:
        copy.wait()


def swap(value):
    return lax.ppermute(value, TM[2], [(0, 1), (1, 0)])


def shift(value, sign):
    count = lax.axis_size("row")
    pairs = []
    for c, step in ((0, sign), (1, -sign)):
        for z in range(count):
            inside = 0 <= z + step < count
            pairs.append((c * count + z, c * count + z + step if inside else (1 - c) * count + z))
    return lax.ppermute(value, (TM[2], "row"), pairs)


def others(value, axis):
    count = lax.axis_size(axis)
    pairs = [[(i, p) for i, p in enumerate(group)] for group in zip(*(
        [int(p) for p in host_partners(i, count)] for i in range(count)
    ))]
    got = []
    for pair in pairs:
        got.append(lax.ppermute(value, axis, pair))
    return got


def host_partners(index, count):
    if count == 2:
        return [1 - index]
    return [(index + 2) % 4, index ^ 1, 3 - index]


def shards(frames, state_in, modulus, angle, w_in, w_out):
    nf, rows, width, chans = frames.shape
    ny, nx, _ = (lax.axis_size(name) for name in TM)
    far, modulus = (pltpu.with_memory_space_constraint(v, pltpu.HBM) for v in (frames, modulus))
    angle = pltpu.with_memory_space_constraint(angle[None], pltpu.HBM)
    conv_flops = 2 * nf * rows * width * 9 * chans * chans
    conv_bytes = 9 * chans * chans * 2

    def shape(*dims, dtype=F32):
        return jax.ShapeDtypeStruct(dims, dtype)

    row_bf = shape(nf, width, chans, dtype=BF16)
    acc_row = shape(nf * width, chans)
    one_row = shape(width, chans)
    one_bf = shape(width, chans, dtype=BF16)
    two_rows = shape(2, nf, width, chans)

    one, two = call(
        edges,
        (row_bf, row_bf),
        [HBM],
        scratch=[pltpu.SemaphoreType.DMA((2,))],
        flops=conv_flops * 10,
        size=20 * conv_bytes,
    )(far)
    got_one, got_two = shift(one, 1), shift(two, -1)

    def pair_steps(own, message, axis, place, keep_last):
        count = lax.axis_size(axis)
        partner = [lambda i: i ^ 1, lambda i: 3 - i][: 1 if count == 2 else 2]
        prefix = []
        for i, of in enumerate(partner):
            got = lax.ppermute(message, axis, [(k, of(k)) for k in range(count)])
            if keep_last and i == len(partner) - 1:
                return got, prefix, place + 3 * i
            goes_on = not (keep_last and i == len(partner) - 2)
            before, message, *total = call(
                functools.partial(
                    join_pair, place=place + 3 * i, first=i == 0, goes_on=goes_on
                ),
                (one_row, one_bf) + (one_row,) * goes_on,
                [VM] * (3 + len(prefix)),
            )(own, got, *prefix, tab)
            own = total[0] if goes_on else None
            prefix = [before]
        return own, message, before

    inner, keep, send, tab = call(
        functools.partial(update_inner, nx=nx, ny=ny),
        (two_rows, one_row, one_row, shape(ROWS, 8, chans)),
        [VM, VM, HBM, HBM],
        scratch=[
            pltpu.VMEM(modulus.shape, F32),
            pltpu.VMEM(angle.shape, F32),
            pltpu.SemaphoreType.DMA((2,)),
        ],
        flops=conv_flops // 2,
        size=conv_bytes,
    )(frames, w_in, modulus, angle)
    got = swap(send)
    acc = call(
        update_outer,
        shape(2, nf * width, chans),
        [VM, VM],
        flops=conv_flops // 3,
        size=conv_bytes,
    )(frames, w_in)
    start, own, message = call(join_cores, (one_row, one_row, one_bf), [VM] * 3)(keep, got, tab)
    own, message, prefix = pair_steps(own, message, TM[1], XPAIR, False)
    got, before, place = pair_steps(own, message, TM[0], YPAIR, True)
    keep_in, send_in = call(
        functools.partial(join_inner, place=place), (one_row, one_row), [VM] * (5 + len(before))
    )(got, *before, prefix, start, state_in, tab)
    got_in = swap(send_in)

    outer, keep, send, one, two = call(
        finish_outer,
        (two_rows, one_row, one_row, row_bf, row_bf),
        [VM] * 5,
        flops=conv_flops // 6,
        size=conv_bytes,
    )(acc, got_one, got_two, w_in, tab)
    got = swap(send)
    got_one, got_two = shift(one, 1), shift(two, -1)
    start, chip = call(join_cores, (one_row, one_bf), [VM] * 3)(keep, got, tab)
    across = others(chip, TM[1])
    prefix, total = call(join_row, (one_row, one_bf), [VM] * (nx + 1))(chip, *across, tab)
    across = others(total, TM[0])
    keep_out, send = call(join_outer, (one_row, one_row), [VM] * (ny + 3))(
        *across, prefix, start, state_in, tab
    )
    got_out = swap(send)
    entry_two = shift(keep_out, -1)
    entry_one = shift(got_out, 1)
    acc_top, acc_bottom, inside = call(
        conv_state,
        (acc_row, acc_row, shape(rows - 2, nf, width, chans, dtype=BF16)),
        [VM] * 8,
        flops=conv_flops * 10 // 12,
        size=conv_bytes,
    )(inner, outer, keep_in, got_in, keep_out, got_out, tab, w_out)
    return call(
        finish_output,
        shape(nf, rows, width, chans, dtype=BF16),
        [VM] * 9,
        out_specs=HBM,
        scratch=[pltpu.VMEM((2, nf, width, chans), BF16), pltpu.SemaphoreType.DMA((rows,))],
        flops=conv_flops // 6,
        size=conv_bytes,
    )(acc_top, acc_bottom, got_one, got_two, entry_one, entry_two, tab, w_out, inside)


def solution(mesh):
    chips = mesh.shape["tm"] // 2
    side = int(chips**0.5)
    finer = Mesh(
        mesh.devices.reshape(chips // side, side, 2, mesh.shape["row"]), (*TM, "row")
    )
    placed = (P(TM, "row", None, None), P("row", None, None), P(), P(), P(), P())

    return jax.shard_map(
        shards, mesh=finer, in_specs=placed, out_specs=P(TM, "row", None, None), check_vma=False
    )
```
